32 devices in a mesh: order: 4 (over y, x), chan: 8 (over z, core).
Axes of the slice: x: 2, y: 2, z: 4, core: 2. Of those that a mesh axis runs over, the one named last changes fastest.
Arguments:
- grad_out: bfloat16 [3, 256, 720, 1440], P(None, 'chan', 'order'), may hold values from -6 to 6
- legendre: bfloat16 [48, 720, 768], P('order', 'chan'), as said below
- filter_re: float32 [256, 720], P('chan'), may hold values from -6 to 6
- filter_im: float32 [256, 720], P('chan'), may hold values from -6 to 6
- quad_weight: float32 [720], P('order'), may hold values from 0.5 to 2
- pair_order: int32 [48], replicated, may hold values from 0 to 359, as said below
Outputs:
- grad_in: bfloat16 [3, 256, 720, 1440], P(None, 'chan', 'order')
The draws below stay inside these ranges and needn't reach their ends.
Inputs may be any that keep to these rules, and one draw needn't show every extreme that they name: `pair_order`: the values are distinct. Slot j belongs to index j // 12 of order. `legendre`: entries in rows r > 720 of the last dimension are zero.
All inputs are finite; a program needn't handle non-finite values.
Results may differ from the reference program's by a relative error of at most 0.0072.
Values may be sent and summed in bfloat16 or wider, within the bound.
A program may use at most 256 MiB of HBM per device.

```python
import math
import jax
import jax.numpy as jnp
from jax import lax

C = 256
NLAT = 720
NLON = 1440
M = 720
SAMPLES = 3
PAIRS = 48
LROWS = 768


def draw_pair_order(key, part):
    return jax.random.permutation(key, M // 2)[:PAIRS].astype(jnp.int32)


def draw_legendre(key, part):
    values = jax.random.normal(key, (PAIRS, NLAT, LROWS), jnp.float32)
    row_ids = jnp.arange(LROWS, dtype=jnp.int32)
    live = (row_ids <= M).astype(jnp.float32)
    return (values * live[None, None, :] * NLAT ** (-0.5)).astype(jnp.bfloat16)


def steps_of(rng, dims, cuts, smallest, top_value):
    level, own = 1.0, jax.random.fold_in(rng, 6)
    for position, blocks in cuts:
        heights = jnp.exp(jax.random.uniform(jax.random.fold_in(own, position), (blocks,), jnp.float32, smallest / len(cuts), top_value / len(cuts)))
        level = level * jnp.repeat(heights, dims[position] // blocks).reshape([-1 if axis == position else 1 for axis in range(len(dims))])
    return level


def normal_values(rng, shape, scale, reach, pieces=(), held_as=jnp.bfloat16):
    factor_of = steps_of(rng, shape, pieces, -0.22, 0.18) if pieces else 1.0
    entries = jax.random.normal(rng, shape, jnp.float32) * scale * factor_of
    return jnp.minimum(jnp.maximum(entries, -reach), reach).astype(held_as)


def setup_inputs(seed: int = 0) -> dict:
    seeds = jax.random.split(jax.random.key(seed), 7)
    return {
        "grad_out": normal_values(seeds[0], (SAMPLES, C, NLAT, NLON), 1.0, 6.0, ((1, 8), (2, 4))),
        "legendre": draw_legendre(jax.random.fold_in(seeds[6], 71), 0),
        "filter_re": normal_values(seeds[2], (C, M), 1.0, 6.0, ((0, 8),), jnp.float32),
        "filter_im": normal_values(seeds[3], (C, M), 1.0, 6.0, ((0, 8),), jnp.float32),
        "quad_weight": jnp.clip(jnp.exp(math.log(2.0) - 1.3862944 * jax.random.uniform(seeds[4], (NLAT,), jnp.float32) ** steps_of(seeds[4], (NLAT,), ((0, 4),), -0.2, 0.2)), 0.5, 2.0),
        "pair_order": draw_pair_order(jax.random.fold_in(seeds[6], 71), 0),
    }


def basis_tables(pair_order):
    low_order = pair_order.astype(jnp.int32)
    high_order = M - 1 - low_order
    orders = jnp.stack([low_order, low_order, high_order, high_order], axis=1).reshape(-1)
    columns = orders.shape[0]
    parity = jnp.arange(columns, dtype=jnp.int32) % 2
    longitude = jnp.arange(NLON, dtype=jnp.int32)
    phases = (longitude[:, None] * orders[None, :]) % NLON
    angles = phases.astype(jnp.float32) * (2.0 * math.pi / NLON)
    fourier = jnp.where(parity[None, :] == 0, jnp.cos(angles), -jnp.sin(angles))
    factor = jnp.where(orders == 0, 1.0, 2.0).astype(jnp.float32)
    forward = (fourier * factor[None, :]).astype(jnp.bfloat16)
    inverse = fourier.T.astype(jnp.bfloat16)
    return forward, inverse


def spectral_masks(low_order):
    row_ids = jnp.arange(LROWS, dtype=jnp.int32)
    below = row_ids[None, :] < (M - low_order)[:, None]
    degree = jnp.where(below, low_order[:, None] + row_ids[None, :], row_ids[None, :] - 1)
    return below, jnp.clip(degree, 0, M - 1).astype(jnp.int32)


def apply_filter(spectrum, low_order, filter_re, filter_im):
    below, degree = spectral_masks(low_order)
    channels = filter_re.shape[0]
    pairs, rows = degree.shape
    gain_re = jnp.take(filter_re, degree.reshape(-1), axis=1).reshape(channels, pairs, rows)
    gain_im = jnp.take(filter_im, degree.reshape(-1), axis=1).reshape(channels, pairs, rows)
    gain_re = jnp.transpose(gain_re, (1, 2, 0))[:, :, None, :]
    gain_im = jnp.transpose(gain_im, (1, 2, 0))[:, :, None, :]
    inside = below[:, :, None, None]
    former = jnp.where(inside, spectrum[..., 0], spectrum[..., 2])
    latter = jnp.where(inside, spectrum[..., 1], spectrum[..., 3])
    real_part = gain_re * former + gain_im * latter
    imag_part = gain_re * latter - gain_im * former
    keep_mask = inside.astype(real_part.dtype)
    split = jnp.stack([real_part * keep_mask, imag_part * keep_mask,
                       real_part * (1.0 - keep_mask), imag_part * (1.0 - keep_mask)], axis=-1)
    return split.astype(jnp.bfloat16)


def reference(grad_out, legendre, filter_re, filter_im, quad_weight, pair_order):
    forward, inverse = basis_tables(pair_order)

    def transform(sample):
        flat = sample.reshape(C * NLAT, NLON)
        result = jnp.dot(flat, forward, preferred_element_type=jnp.float32).astype(jnp.bfloat16)
        return result.reshape(C, NLAT, PAIRS, 4)

    coeffs = lax.map(transform, grad_out)
    per_slot = jnp.transpose(coeffs, (3, 0, 1, 2, 4))

    def one_slot(inputs):
        table, block, lowest = inputs
        spectrum = jnp.einsum("tr,sctq->rscq", table.astype(jnp.float32), block.astype(jnp.float32))
        split = apply_filter(spectrum[None], lowest[None], filter_re, filter_im)[0]
        synth = jnp.einsum("tr,rscq->sctq", table.astype(jnp.float32), split.astype(jnp.float32))
        return synth.astype(jnp.bfloat16)

    synthesis = lax.map(one_slot, (legendre, per_slot, pair_order.astype(jnp.int32)))
    synthesis = jnp.transpose(synthesis, (1, 2, 3, 0, 4)).reshape(SAMPLES, C * NLAT, PAIRS * 4)

    def back(block):
        return jnp.dot(block, inverse, preferred_element_type=jnp.float32)

    values = lax.map(back, synthesis).reshape(SAMPLES, C, NLAT, NLON)
    scale = quad_weight * (2.0 * math.pi / NLON)
    return (values * scale[None, None, :, None]).astype(jnp.bfloat16)
```

```python
import functools
import math

import jax
import jax.numpy as jnp
from jax import lax
from jax.experimental import pallas as pl
from jax.experimental.pallas import tpu as pltpu
from jax.sharding import PartitionSpec as P

NLON = 1440
M = 720
TILE = 16
MESH = pl.DeviceIdType.MESH


def step_of(count, most):
    return max(d for d in range(1, most + 1) if count % d == 0)


def basis_tables(pair_order):
    low = pair_order
    orders = jnp.stack([low, low, M - 1 - low, M - 1 - low], axis=1).reshape(-1)
    columns = orders.shape[0]
    real = jnp.arange(columns, dtype=jnp.int32) % 2 == 0
    longitude = jnp.arange(NLON, dtype=jnp.int32)

    def table(phases, real):
        angles = (phases % NLON).astype(jnp.float32) * (2.0 * math.pi / NLON)
        return jnp.where(real, jnp.cos(angles), -jnp.sin(angles))

    inverse = table(orders[:, None] * longitude[None, :], real[:, None])
    factor = jnp.where(orders == 0, 1.0, 2.0).astype(jnp.float32)
    forward = (inverse * factor[:, None]).astype(jnp.bfloat16)
    wide = -(-columns // 128) * 128
    forward = jnp.pad(forward, ((0, wide - columns), (0, 0))).T
    inverse = inverse.astype(jnp.bfloat16).reshape(-1, 4, NLON)
    return forward, jnp.transpose(inverse, (1, 0, 2)).reshape(columns, NLON)


class Line:
    def __init__(self, chips, first, pairs, groups, source, table, sems):
        self.chips, self.first, self.pairs, self.groups = chips, first, pairs, groups
        self.source, self.table = source, table
        self.up_recv, self.down_recv, self.flags = sems
        self.index = lax.axis_index("chan")
        self.place = self.index // 2
        self.partner = self.index + 1 - 2 * (self.index % 2)
        self.share = pairs // groups

    def remote(self, src, dst, send, recv, target):
        return pltpu.make_async_remote_copy(
            src_ref=src, dst_ref=dst, send_sem=send, recv_sem=recv, device_id={"chan": target}, device_id_type=MESH
        )

    def own(self):
        src = self.source.at[pl.ds(self.first, self.pairs)]
        return pltpu.make_async_copy(src, self.table.at[:, self.index], self.flags.at[0])

    def start(self):
        self.own().start()
        src = self.source.at[pl.ds(self.first, self.pairs)]
        self.remote(src, self.table.at[:, self.index], self.flags.at[1], self.flags.at[2], self.partner).start()
        for group in range(self.groups):
            src = self.source.at[pl.ds(self.first + group * self.share, self.share)]
            dst = self.table.at[pl.ds(group * self.share, self.share), self.index]

            @pl.when(self.place < self.chips - 1)
            def _():
                self.remote(src, dst, self.flags.at[3], self.up_recv.at[0, group], self.index + 2).start()

            @pl.when(self.place > 0)
            def _():
                self.remote(src, dst, self.flags.at[4], self.down_recv.at[0, group], self.index - 2).start()

    def step(self, hop, group):
        rows = pl.ds(group * self.share, self.share)

        @pl.when(self.place >= hop)
        def _():
            block = self.table.at[rows, self.index - 2 * hop]
            self.remote(block, block, self.flags.at[3], self.up_recv.at[hop - 1, group], self.index - 2).wait_recv()

            @pl.when(self.place < self.chips - 1)
            def _():
                self.remote(block, block, self.flags.at[3], self.up_recv.at[hop, group], self.index + 2).start()

            self.remote(block, block, self.flags.at[1], self.flags.at[2], self.partner).start()

        @pl.when(self.place + hop < self.chips)
        def _():
            block = self.table.at[rows, self.index + 2 * hop]
            self.remote(block, block, self.flags.at[4], self.down_recv.at[hop - 1, group], self.index + 2).wait_recv()

            @pl.when(self.place > 0)
            def _():
                self.remote(block, block, self.flags.at[4], self.down_recv.at[hop, group], self.index - 2).start()

            self.remote(block, block, self.flags.at[1], self.flags.at[2], self.partner).start()

    def finish(self):
        self.own().wait()
        total = self.table.at[:, pl.ds(0, self.chips)]
        every = self.remote(total, total, self.flags.at[1], self.flags.at[2], self.partner)
        every.wait_send()
        every.wait_recv()
        for place in range(self.chips):
            if place < self.chips - 1:

                @pl.when(self.place == place)
                def _():
                    part = self.table.at[:, pl.ds(0, place + 1)]
                    self.remote(part, part, self.flags.at[3], self.flags.at[2], self.partner).wait_send()

            if place > 0:

                @pl.when(self.place == place)
                def _():
                    part = self.table.at[:, pl.ds(0, self.chips - place)]
                    self.remote(part, part, self.flags.at[4], self.flags.at[2], self.partner).wait_send()


def enter(devices, chips):
    order = lax.axis_index("order")
    index = lax.axis_index("chan")
    place = index // 2
    barrier = pltpu.get_barrier_semaphore()
    for turn in range(1, devices):
        peer = lax.rem(order + turn, devices)
        pl.semaphore_signal(barrier, inc=1, device_id={"order": peer}, device_id_type=MESH)
    partner = index + 1 - 2 * (index % 2)
    pl.semaphore_signal(barrier, inc=1, device_id={"chan": partner}, device_id_type=MESH)

    @pl.when(place < chips - 1)
    def _():
        pl.semaphore_signal(barrier, inc=1, device_id={"chan": index + 2}, device_id_type=MESH)

    @pl.when(place > 0)
    def _():
        pl.semaphore_signal(barrier, inc=1, device_id={"chan": index - 2}, device_id_type=MESH)

    near = jnp.minimum(place, 1) + jnp.minimum(chips - 1 - place, 1)
    pl.semaphore_wait(barrier, devices + near)


def to_order(src, dst, send, recv, peer):
    return pltpu.make_async_remote_copy(
        src_ref=src, dst_ref=dst, send_sem=send, recv_sem=recv, device_id={"order": peer}, device_id_type=MESH
    )


def forward_kernel(
    x_ref, table_ref, legendre_ref, out_ref, gathered_ref, x_buf, turned_ref, stage_ref,
    x_sem, send_sem, recv_sem, own_sem, up_sem, down_sem, flag_sem, *, devices, chips, groups, block_rows
):
    samples, lat_local, channels, _ = x_ref.shape
    pairs, blocks, padded, lanes = out_ref.shape
    sc = samples * channels
    order = lax.axis_index("order")
    per_band = blocks // devices
    per_block = padded // TILE
    chunks = per_band * per_block
    slack = max(0, (per_band - 1) * block_rows + padded - lat_local)
    line = Line(chips, 0, gathered_ref.shape[0], groups, legendre_ref, gathered_ref, (up_sem, down_sem, flag_sem))

    def x_copy(chunk):
        start = (chunk // per_block) * block_rows + (chunk % per_block) * TILE
        back = jnp.maximum(start + TILE - lat_local, 0)
        slot = chunk % 2
        return pltpu.make_async_copy(
            x_ref.at[:, pl.ds(start - back, TILE)], x_buf.at[slot, :, pl.ds(slack - back, TILE)], x_sem.at[slot]
        )

    x_copy(0).start()
    enter(devices, chips)
    line.start()
    steps = (chips - 1) * groups

    def body(chunk, carry):
        slot = chunk % 2
        x_copy(chunk).wait()

        @pl.when(chunk + 1 < chunks)
        def _():
            x_copy(chunk + 1).start()

        pieces = [x_buf[slot, s, slack + t] for t in range(TILE) for s in range(samples)]
        coeffs = jnp.dot(jnp.concatenate(pieces, axis=0), table_ref[...], preferred_element_type=jnp.float32)
        for t in range(TILE):
            turned = coeffs[t * sc : (t + 1) * sc].T
            turned_ref[t, :, 0:sc] = turned[: turned_ref.shape[1]]
        block, part = chunk // per_block, chunk % per_block
        live = lax.broadcasted_iota(jnp.int32, (TILE, lanes), 0) < block_rows - part * TILE
        for pair in range(devices * pairs):
            row = jnp.concatenate([turned_ref[:, 4 * pair + q, 0:sc] for q in range(4)], axis=1)
            stage_ref[chunk, pair] = jnp.where(live, row, 0.0).astype(jnp.bfloat16)
        target = out_ref.at[:, order * per_band + block, pl.ds(part * TILE, TILE)]
        for turn in range(1, devices):
            peer = lax.rem(order + turn, devices)
            src = stage_ref.at[chunk, pl.ds(peer * pairs, pairs)]
            to_order(src, target, send_sem.at[turn], recv_sem.at[turn], peer).start()
        pltpu.make_async_copy(stage_ref.at[chunk, pl.ds(order * pairs, pairs)], target, own_sem).start()
        step = chunk - 1

        @pl.when((step >= 0) & (step < steps))
        def _():
            line.step(step // groups + 1, step % groups)

        return carry

    lax.fori_loop(0, chunks, body, 0)
    if steps > chunks - 1:

        def rest(step, carry):
            line.step(step // groups + 1, step % groups)
            return carry

        lax.fori_loop(chunks - 1, steps, rest, 0)
    for turn in range(1, devices):
        peer = lax.rem(order + turn, devices)
        source = lax.rem(order + devices - turn, devices)
        sent = out_ref.at[:, pl.ds(peer * per_band, per_band)]
        got = out_ref.at[:, pl.ds(source * per_band, per_band)]
        both = to_order(sent, got, send_sem.at[turn], recv_sem.at[turn], peer)
        both.wait_send()
        both.wait_recv()
    own = out_ref.at[:, pl.ds(order * per_band, per_band)]
    pltpu.make_async_copy(own, own, own_sem).wait()
    line.finish()


def middle_kernel(
    low_ref, coeffs_ref, early_ref, legendre_ref, gains_ref, shifted_ref, out_ref, late_ref, z_buf, l_buf, stage_ref,
    z_sem, l_sem, send_sem, recv_sem, own_sem, up_sem, down_sem, flag_sem, *, devices, chips, groups, samples
):
    pairs, blocks, padded, lanes = coeffs_ref.shape
    packed_rows = legendre_ref.shape[2]
    early = early_ref.shape[0]
    rows = blocks * padded
    band = rows // devices
    half = lanes // 2
    sc = half // 2
    channels = sc // samples
    order = lax.axis_index("order")
    line = Line(chips, early, pairs - early, groups, legendre_ref, late_ref, (up_sem, down_sem, flag_sem))

    def z_copy(pair):
        return pltpu.make_async_copy(coeffs_ref.at[pair], z_buf.at[pair % 2], z_sem.at[pair % 2])

    def l_copy(ref, entry, slot):
        return pltpu.make_async_copy(ref.at[entry], l_buf.at[slot], l_sem.at[slot])

    z_copy(0).start()
    l_copy(early_ref, 0, 0).start()
    enter(devices, chips)
    line.start()
    steps = (chips - 1) * groups
    contract = (((0,), (0,)), ((), ()))
    row_ids = lax.broadcasted_iota(jnp.int32, (packed_rows, half), 0)

    def body(pair, carry):
        slot = pair % 2
        z_copy(pair).wait()
        l_copy(early_ref, 0, slot).wait()

        @pl.when(pair + 1 < pairs)
        def _():
            z_copy(pair + 1).start()

        @pl.when(pair + 1 < early)
        def _():
            l_copy(early_ref, pair + 1, 1 - slot).start()

        @pl.when((pair + 1 >= early + 1) & (pair + 1 < pairs))
        def _():
            l_copy(late_ref, pair + 1 - early, 1 - slot).start()

        legendre = l_buf[slot].reshape(rows, packed_rows)
        coeffs = z_buf[slot].reshape(rows, lanes)
        spectrum = lax.dot_general(legendre, coeffs, contract, preferred_element_type=jnp.float32)
        low = low_ref[pair]
        inside = row_ids < M - low
        own = jnp.where(inside, spectrum[:, :half], spectrum[:, half:])
        other = jnp.concatenate([own[:, sc:], own[:, :sc]], axis=1)
        gains = jnp.where(inside[:, : 2 * channels], gains_ref[pl.ds(low, packed_rows), :], shifted_ref[...])
        gain_re = gains[:, :channels]
        gain_im = gains[:, channels:]
        gain_re = jnp.concatenate([gain_re] * (2 * samples), axis=1)
        gain_im = jnp.concatenate([gain_im] * samples + [-gain_im] * samples, axis=1)
        filtered = gain_re * own + gain_im * other
        zeros = jnp.zeros_like(filtered)
        split = jnp.concatenate([jnp.where(inside, filtered, zeros), jnp.where(inside, zeros, filtered)], axis=1)
        synthesis = jnp.dot(legendre, split.astype(jnp.bfloat16), preferred_element_type=jnp.float32)
        stage_ref[pair] = synthesis.astype(jnp.bfloat16)
        target = out_ref.at[order, pair]
        for turn in range(1, devices):
            peer = lax.rem(order + turn, devices)
            src = stage_ref.at[pair, pl.ds(peer * band, band)]
            to_order(src, target, send_sem.at[turn], recv_sem.at[turn], peer).start()
        pltpu.make_async_copy(stage_ref.at[pair, pl.ds(order * band, band)], target, own_sem).start()

        @pl.when(pair + 1 == early)
        def _():
            def gather(step, carry):
                line.step(step // groups + 1, step % groups)
                return carry

            lax.fori_loop((early - 1) // 2, steps, gather, 0)
            line.finish()
            l_copy(late_ref, 0, 1 - slot).start()

        @pl.when((pair + 1 < early) & (pair % 2 == 1) & (pair // 2 < steps))
        def _():
            step = pair // 2
            line.step(step // groups + 1, step % groups)

        return carry

    lax.fori_loop(0, pairs, body, 0)
    for turn in range(1, devices):
        peer = lax.rem(order + turn, devices)
        source = lax.rem(order + devices - turn, devices)
        both = to_order(out_ref.at[peer], out_ref.at[source], send_sem.at[turn], recv_sem.at[turn], peer)
        both.wait_send()
        both.wait_recv()
    pltpu.make_async_copy(out_ref.at[order], out_ref.at[order], own_sem).wait()


def inverse_kernel(scale_ref, band_ref, table_ref, out_ref, wide_ref):
    count, padded, lanes = band_ref.shape
    samples, steps, channels, longitudes = out_ref.shape
    sc = samples * channels
    block, part = pl.program_id(0), pl.program_id(1)

    @pl.when(part == 0)
    def _():
        def spread(pair, carry):
            wide_ref[pair] = band_ref[pair].astype(jnp.float32)
            return carry

        lax.fori_loop(0, count, spread, 0)

    pieces = []
    for t in range(steps):
        rows = wide_ref[:, part * steps + t].astype(jnp.bfloat16)
        pieces.append(jnp.concatenate([rows[:, q * sc : (q + 1) * sc] for q in range(4)], axis=0).T)
    values = jnp.dot(jnp.concatenate(pieces, axis=0), table_ref[...], preferred_element_type=jnp.float32)
    start = (block * pl.num_programs(1) + part) * steps
    for t in range(steps):
        scale = scale_ref[start + t]
        for s in range(samples):
            row = t * sc + s * channels
            out_ref[s, t] = (values[row : row + channels] * scale).astype(jnp.bfloat16)


def body(grad_out, legendre, filter_re, filter_im, quad_weight, pair_order, *, devices, members):
    samples, channels, lat_local, longitudes = grad_out.shape
    pairs, block_rows, packed_rows = legendre.shape
    lanes = 4 * samples * channels
    padded = -(-block_rows // TILE) * TILE
    per_band = lat_local // block_rows
    chips = members // 2
    columns = devices * pairs * 4
    early = (2 * pairs) // 3
    early_groups = step_of(early, 4)
    late_groups = step_of(pairs - early, 2)
    forward, inverse = basis_tables(pair_order)
    legendre = jnp.pad(legendre, ((0, 0), (0, padded - block_rows), (0, 0)))
    hbm = pl.BlockSpec(memory_space=pl.ANY)
    vmem = pl.BlockSpec(memory_space=pltpu.VMEM)
    smem = pl.BlockSpec(memory_space=pltpu.SMEM)
    bf16 = jnp.bfloat16
    dma = pltpu.SemaphoreType.DMA
    chunks = per_band * padded // TILE
    slack = max(0, (per_band - 1) * block_rows + padded - lat_local)

    def params(collective_id):
        return pltpu.CompilerParams(
            collective_id=collective_id, has_side_effects=True, vmem_limit_bytes=60 << 20
        )

    def line_sems(groups):
        return [dma((chips, groups)), dma((chips, groups)), dma((5,))]

    coeffs, early_table = pl.pallas_call(
        functools.partial(
            forward_kernel, devices=devices, chips=chips, groups=early_groups, block_rows=block_rows
        ),
        in_specs=[hbm, vmem, vmem],
        out_specs=[hbm, hbm],
        out_shape=[
            jax.ShapeDtypeStruct((pairs, members, padded, lanes), bf16),
            jax.ShapeDtypeStruct((early, members, padded, packed_rows), bf16),
        ],
        scratch_shapes=[
            pltpu.VMEM((2, samples, TILE + slack, channels, longitudes), bf16),
            pltpu.VMEM((TILE, columns, -(-(samples * channels) // 128) * 128), jnp.float32),
            pltpu.VMEM((chunks, devices * pairs, TILE, lanes), bf16),
            dma((2,)), dma((devices,)), dma((devices,)), dma, *line_sems(early_groups),
        ],
        compiler_params=params(0),
        name="fourier",
    )(jnp.transpose(grad_out, (0, 2, 1, 3)), forward, legendre)

    start_slot = lax.axis_index("order") * pairs
    low_order = lax.dynamic_slice_in_dim(pair_order, start_slot, pairs)
    both = jnp.concatenate([filter_re, filter_im], axis=0).T
    gains = jnp.pad(both, ((0, packed_rows), (0, 0)))
    tail = jnp.broadcast_to(both[M - 1 : M], (packed_rows - 1 - M, both.shape[1]))
    shifted = jnp.concatenate([both[:1], both, tail], axis=0)
    band, _ = pl.pallas_call(
        functools.partial(middle_kernel, devices=devices, chips=chips, groups=late_groups, samples=samples),
        in_specs=[smem, hbm, hbm, vmem, vmem, vmem],
        out_specs=[hbm, hbm],
        out_shape=[
            jax.ShapeDtypeStruct((devices, pairs, per_band * padded, lanes), bf16),
            jax.ShapeDtypeStruct((pairs - early, members, padded, packed_rows), bf16),
        ],
        scratch_shapes=[
            pltpu.VMEM((2, members, padded, lanes), bf16),
            pltpu.VMEM((2, members, padded, packed_rows), bf16),
            pltpu.VMEM((pairs, members * padded, lanes), bf16),
            dma((2,)), dma((2,)), dma((devices,)), dma((devices,)), dma, *line_sems(late_groups),
        ],
        compiler_params=params(1),
        name="legendre",
    )(low_order, coeffs, early_table, legendre, gains, shifted)

    scale = quad_weight * (2.0 * math.pi / NLON)
    steps = step_of(block_rows, 10)
    parts = block_rows // steps
    values = pl.pallas_call(
        inverse_kernel,
        grid=(per_band, parts),
        in_specs=[
            smem,
            pl.BlockSpec((devices * pairs, padded, lanes), lambda b, i: (0, b, 0)),
            pl.BlockSpec((columns, longitudes), lambda b, i: (0, 0)),
        ],
        out_specs=pl.BlockSpec((samples, steps, channels, longitudes), lambda b, i: (0, b * parts + i, 0, 0)),
        out_shape=jax.ShapeDtypeStruct((samples, lat_local, channels, longitudes), bf16),
        scratch_shapes=[pltpu.VMEM((devices * pairs, padded, lanes), jnp.float32)],
        compiler_params=pltpu.CompilerParams(
            dimension_semantics=("arbitrary", "arbitrary"), vmem_limit_bytes=56 << 20
        ),
        name="fourier_back",
    )(scale, band.reshape(devices * pairs, per_band * padded, lanes), inverse)
    return jnp.transpose(values, (0, 2, 1, 3))


def solution(mesh):
    in_specs = (
        P(None, "chan", "order", None),
        P("order", "chan", None),
        P("chan", None),
        P("chan", None),
        P("order"),
        P(),
    )
    out_specs = P(None, "chan", "order", None)
    local = functools.partial(body, devices=mesh.shape["order"], members=mesh.shape["chan"])
    return jax.shard_map(local, mesh=mesh, in_specs=in_specs, out_specs=out_specs, check_vma=False)
```

```python
import functools
import math

import jax
import jax.numpy as jnp
from jax import lax
from jax.experimental import pallas as pl
from jax.experimental.pallas import tpu as pltpu
from jax.sharding import PartitionSpec as P

NLON = 1440
M = 720
TILE = 16
FINE = 32
HEAD = 8
MESH = pl.DeviceIdType.MESH


def step_of(count, most):
    return max(d for d in range(1, most + 1) if count % d == 0)


def order_lanes(low_ref, sequence, width):
    count = len(sequence)
    lane = lax.broadcasted_iota(jnp.int32, (1, width), 1)
    turn = sum((lane >= q * count).astype(jnp.int32) for q in range(1, 5))
    place = lane - turn * count
    low = jnp.zeros((1, width), jnp.float32)
    for index, pair in enumerate(sequence):
        low = jnp.where(place == index, low_ref[pair].astype(jnp.float32), low)
    orders = jnp.where(turn < 2, low, (M - 1) - low)
    return orders, (turn == 0) | (turn == 2), turn < 4


def circle(phases):
    phases = phases - NLON * jnp.floor(phases * (1.0 / NLON))
    angles = phases * (2.0 * math.pi / NLON)
    return jnp.cos(angles), jnp.sin(angles)


def iota(shape, axis):
    return lax.broadcasted_iota(jnp.int32, shape, axis).astype(jnp.float32)


def fill_forward(low_ref, table_ref, count):
    width = table_ref.shape[1]
    orders, real, live = order_lanes(low_ref, range(count), width)
    coarse_cos, coarse_sin = circle(iota((NLON // FINE, width), 0) * FINE * orders)
    fine_cos, fine_sin = circle(iota((FINE, width), 0) * orders)
    factor = jnp.where(orders == 0.0, 1.0, 2.0) * jnp.where(live, 1.0, 0.0)
    first = jnp.where(real, coarse_cos, -coarse_sin) * factor
    second = jnp.where(real, -coarse_sin, -coarse_cos) * factor
    for part in range(NLON // FINE):
        rows = first[part : part + 1] * fine_cos + second[part : part + 1] * fine_sin
        table_ref[part * FINE : (part + 1) * FINE] = rows.astype(jnp.bfloat16)


def fill_inverse(low_ref, table_ref, sequence):
    columns = table_ref.shape[0]
    width = -(-columns // 128) * 128
    orders, real, _ = order_lanes(low_ref, sequence, width)
    orders = jnp.broadcast_to(orders, (128, width)).T[:columns]
    real = jnp.broadcast_to(jnp.where(real, 1.0, 0.0), (128, width)).T[:columns] > 0.5
    fine_cos, fine_sin = circle(iota((columns, 128), 1) * orders)
    coarse_cos, coarse_sin = circle(iota((columns, 128), 1) * 128.0 * orders)
    first = jnp.where(real, coarse_cos, -coarse_sin)
    second = jnp.where(real, -coarse_sin, -coarse_cos)
    for start in range(0, NLON, 128):
        part = start // 128
        values = first[:, part : part + 1] * fine_cos + second[:, part : part + 1] * fine_sin
        size = min(128, NLON - start)
        table_ref[:, start : start + size] = values[:, :size].astype(jnp.bfloat16)


class Line:
    def __init__(self, chips, first, pairs, groups, source, table, sems):
        self.chips, self.first, self.pairs, self.groups = chips, first, pairs, groups
        self.source, self.table = source, table
        self.up_recv, self.down_recv, self.flags = sems
        self.index = lax.axis_index("chan")
        self.place = self.index // 2
        self.partner = self.index + 1 - 2 * (self.index % 2)
        self.share = pairs // groups

    def remote(self, src, dst, send, recv, target):
        return pltpu.make_async_remote_copy(
            src_ref=src, dst_ref=dst, send_sem=send, recv_sem=recv, device_id={"chan": target}, device_id_type=MESH
        )

    def own(self):
        src = self.source.at[pl.ds(self.first, self.pairs)]
        return pltpu.make_async_copy(src, self.table.at[:, self.index], self.flags.at[0])

    def start(self):
        self.own().start()
        src = self.source.at[pl.ds(self.first, self.pairs)]
        self.remote(src, self.table.at[:, self.index], self.flags.at[1], self.flags.at[2], self.partner).start()
        for group in range(self.groups):
            src = self.source.at[pl.ds(self.first + group * self.share, self.share)]
            dst = self.table.at[pl.ds(group * self.share, self.share), self.index]

            @pl.when(self.place < self.chips - 1)
            def _():
                self.remote(src, dst, self.flags.at[3], self.up_recv.at[0, group], self.index + 2).start()

            @pl.when(self.place > 0)
            def _():
                self.remote(src, dst, self.flags.at[4], self.down_recv.at[0, group], self.index - 2).start()

    def step(self, hop, group):
        rows = pl.ds(group * self.share, self.share)

        @pl.when(self.place >= hop)
        def _():
            block = self.table.at[rows, self.index - 2 * hop]
            self.remote(block, block, self.flags.at[3], self.up_recv.at[hop - 1, group], self.index - 2).wait_recv()

            @pl.when(self.place < self.chips - 1)
            def _():
                self.remote(block, block, self.flags.at[3], self.up_recv.at[hop, group], self.index + 2).start()

            self.remote(block, block, self.flags.at[1], self.flags.at[2], self.partner).start()

        @pl.when(self.place + hop < self.chips)
        def _():
            block = self.table.at[rows, self.index + 2 * hop]
            self.remote(block, block, self.flags.at[4], self.down_recv.at[hop - 1, group], self.index + 2).wait_recv()

            @pl.when(self.place > 0)
            def _():
                self.remote(block, block, self.flags.at[4], self.down_recv.at[hop, group], self.index - 2).start()

            self.remote(block, block, self.flags.at[1], self.flags.at[2], self.partner).start()

    def finish(self):
        self.own().wait()
        total = self.table.at[:, pl.ds(0, self.chips)]
        every = self.remote(total, total, self.flags.at[1], self.flags.at[2], self.partner)
        every.wait_send()
        every.wait_recv()
        for place in range(self.chips):
            if place < self.chips - 1:

                @pl.when(self.place == place)
                def _():
                    part = self.table.at[:, pl.ds(0, place + 1)]
                    self.remote(part, part, self.flags.at[3], self.flags.at[2], self.partner).wait_send()

            if place > 0:

                @pl.when(self.place == place)
                def _():
                    part = self.table.at[:, pl.ds(0, self.chips - place)]
                    self.remote(part, part, self.flags.at[4], self.flags.at[2], self.partner).wait_send()


def enter(devices, chips):
    order = lax.axis_index("order")
    index = lax.axis_index("chan")
    place = index // 2
    barrier = pltpu.get_barrier_semaphore()
    for turn in range(1, devices):
        peer = lax.rem(order + turn, devices)
        pl.semaphore_signal(barrier, inc=1, device_id={"order": peer}, device_id_type=MESH)
    partner = index + 1 - 2 * (index % 2)
    pl.semaphore_signal(barrier, inc=1, device_id={"chan": partner}, device_id_type=MESH)

    @pl.when(place < chips - 1)
    def _():
        pl.semaphore_signal(barrier, inc=1, device_id={"chan": index + 2}, device_id_type=MESH)

    @pl.when(place > 0)
    def _():
        pl.semaphore_signal(barrier, inc=1, device_id={"chan": index - 2}, device_id_type=MESH)

    near = jnp.minimum(place, 1) + jnp.minimum(chips - 1 - place, 1)
    pl.semaphore_wait(barrier, devices + near)


def to_order(src, dst, send, recv, peer):
    return pltpu.make_async_remote_copy(
        src_ref=src, dst_ref=dst, send_sem=send, recv_sem=recv, device_id={"order": peer}, device_id_type=MESH
    )


def forward_kernel(
    low_ref, x_ref, legendre_ref, out_ref, gathered_ref, x_buf, table_ref, turned_ref, stage_ref,
    x_sem, send_sem, recv_sem, own_sem, up_sem, down_sem, flag_sem, *, devices, chips, groups, block_rows
):
    samples, lat_local, channels, _ = x_ref.shape
    pairs, blocks, padded, lanes = out_ref.shape
    sc = samples * channels
    order = lax.axis_index("order")
    per_band = blocks // devices
    per_block = padded // TILE
    chunks = per_band * per_block
    slack = max(0, (per_band - 1) * block_rows + padded - lat_local)
    line = Line(chips, 0, gathered_ref.shape[0], groups, legendre_ref, gathered_ref, (up_sem, down_sem, flag_sem))

    def x_copy(chunk):
        start = (chunk // per_block) * block_rows + (chunk % per_block) * TILE
        back = jnp.maximum(start + TILE - lat_local, 0)
        slot = chunk % 2
        return pltpu.make_async_copy(
            x_ref.at[:, pl.ds(start - back, TILE)], x_buf.at[slot, :, pl.ds(slack - back, TILE)], x_sem.at[slot]
        )

    x_copy(0).start()
    enter(devices, chips)
    line.start()
    steps = (chips - 1) * groups
    count = devices * pairs
    fill_forward(low_ref, table_ref, count)

    def body(chunk, carry):
        slot = chunk % 2
        x_copy(chunk).wait()

        @pl.when(chunk + 1 < chunks)
        def _():
            x_copy(chunk + 1).start()

        pieces = [x_buf[slot, s, slack + t] for t in range(TILE) for s in range(samples)]
        coeffs = jnp.dot(jnp.concatenate(pieces, axis=0), table_ref[...], preferred_element_type=jnp.float32)
        for t in range(TILE):
            turned = coeffs[t * sc : (t + 1) * sc].T
            turned_ref[t, :, 0:sc] = turned[: turned_ref.shape[1]]
        block, part = chunk // per_block, chunk % per_block
        live = lax.broadcasted_iota(jnp.int32, (TILE, lanes), 0) < block_rows - part * TILE
        for pair in range(count):
            row = jnp.concatenate([turned_ref[:, q * count + pair, 0:sc] for q in range(4)], axis=1)
            stage_ref[chunk, pair] = jnp.where(live, row, 0.0).astype(jnp.bfloat16)
        target = out_ref.at[:, order * per_band + block, pl.ds(part * TILE, TILE)]
        for turn in range(1, devices):
            peer = lax.rem(order + turn, devices)
            src = stage_ref.at[chunk, pl.ds(peer * pairs, pairs)]
            to_order(src, target, send_sem.at[turn], recv_sem.at[turn], peer).start()
        pltpu.make_async_copy(stage_ref.at[chunk, pl.ds(order * pairs, pairs)], target, own_sem).start()
        step = chunk - 1

        @pl.when((step >= 0) & (step < steps))
        def _():
            line.step(step // groups + 1, step % groups)

        return carry

    lax.fori_loop(0, chunks, body, 0)
    if steps > chunks - 1:

        def rest(step, carry):
            line.step(step // groups + 1, step % groups)
            return carry

        lax.fori_loop(chunks - 1, steps, rest, 0)
    for turn in range(1, devices):
        peer = lax.rem(order + turn, devices)
        source = lax.rem(order + devices - turn, devices)
        sent = out_ref.at[:, pl.ds(peer * per_band, per_band)]
        got = out_ref.at[:, pl.ds(source * per_band, per_band)]
        both = to_order(sent, got, send_sem.at[turn], recv_sem.at[turn], peer)
        both.wait_send()
        both.wait_recv()
    own = out_ref.at[:, pl.ds(order * per_band, per_band)]
    pltpu.make_async_copy(own, own, own_sem).wait()
    line.finish()


def middle_kernel(
    low_ref, coeffs_ref, early_ref, legendre_ref, filter_re_ref, filter_im_ref, out_ref, inverse_ref, late_ref,
    z_buf, l_buf, gains_ref, stage_ref, band_buf, wide_ref, rows_buf,
    z_sem, l_sem, send_sem, recv_sem, own_sem, out_sem, up_sem, down_sem, flag_sem,
    *, devices, chips, groups, samples, sequence
):
    pairs, blocks, padded, lanes = coeffs_ref.shape
    packed_rows = legendre_ref.shape[2]
    early = early_ref.shape[0]
    rows = blocks * padded
    band = rows // devices
    half = lanes // 2
    sc = half // 2
    channels = sc // samples
    order = lax.axis_index("order")
    line = Line(chips, early, pairs - early, groups, legendre_ref, late_ref, (up_sem, down_sem, flag_sem))

    def z_copy(pair):
        return pltpu.make_async_copy(coeffs_ref.at[pair], z_buf.at[pair % 2], z_sem.at[pair % 2])

    def l_copy(ref, entry, slot):
        return pltpu.make_async_copy(ref.at[entry], l_buf.at[slot], l_sem.at[slot])

    z_copy(0).start()
    l_copy(early_ref, 0, 0).start()
    enter(devices, chips)
    line.start()
    steps = (chips - 1) * groups
    sets, share, lat_local = out_ref.shape[0], out_ref.shape[2] // devices, out_ref.shape[1]
    degrees = filter_re_ref.shape[1]
    filters = jnp.concatenate([filter_re_ref[...], filter_im_ref[...]], axis=0)
    filters = jnp.concatenate([filters, jnp.zeros((2 * channels, packed_rows - degrees), jnp.float32)], axis=1).T
    gains_ref[HEAD : HEAD + packed_rows] = filters
    gains_ref[HEAD + packed_rows :] = jnp.zeros((degrees, 2 * channels), jnp.float32)
    gains_ref[HEAD - 1 : HEAD] = filters[0:1]
    contract = (((0,), (0,)), ((), ()))
    row_ids = lax.broadcasted_iota(jnp.int32, (packed_rows, half), 0)

    def body(pair, carry):
        slot = pair % 2
        z_copy(pair).wait()
        l_copy(early_ref, 0, slot).wait()

        @pl.when(pair + 1 < pairs)
        def _():
            z_copy(pair + 1).start()

        @pl.when(pair + 1 < early)
        def _():
            l_copy(early_ref, pair + 1, 1 - slot).start()

        @pl.when((pair + 1 >= early + 1) & (pair + 1 < pairs))
        def _():
            l_copy(late_ref, pair + 1 - early, 1 - slot).start()

        legendre = l_buf[slot].reshape(rows, packed_rows)
        coeffs = z_buf[slot].reshape(rows, lanes)
        spectrum = lax.dot_general(legendre, coeffs, contract, preferred_element_type=jnp.float32)
        low = low_ref[order * pairs + pair]
        inside = row_ids < M - low
        own = jnp.where(inside, spectrum[:, :half], spectrum[:, half:])
        other = jnp.concatenate([own[:, sc:], own[:, :sc]], axis=1)
        upper = gains_ref[pl.ds(low + HEAD, packed_rows), :]
        gains = jnp.where(inside[:, : 2 * channels], upper, gains_ref[pl.ds(HEAD - 1, packed_rows), :])
        gain_re = gains[:, :channels]
        gain_im = gains[:, channels:]
        gain_re = jnp.concatenate([gain_re] * (2 * samples), axis=1)
        gain_im = jnp.concatenate([gain_im] * samples + [-gain_im] * samples, axis=1)
        filtered = gain_re * own + gain_im * other
        zeros = jnp.zeros_like(filtered)
        split = jnp.concatenate([jnp.where(inside, filtered, zeros), jnp.where(inside, zeros, filtered)], axis=1)
        synthesis = jnp.dot(legendre, split.astype(jnp.bfloat16), preferred_element_type=jnp.float32)
        stage_ref[pair] = synthesis.astype(jnp.bfloat16)
        bundle = pair // share
        target = band_buf.at[bundle, order, pair % share]
        for turn in range(1, devices):
            peer = lax.rem(order + turn, devices)
            src = stage_ref.at[pair, pl.ds(peer * band, band)]
            to_order(src, target, send_sem.at[turn], recv_sem.at[turn, bundle], peer).start()
        pltpu.make_async_copy(stage_ref.at[pair, pl.ds(order * band, band)], target, own_sem.at[bundle]).start()

        @pl.when(pair + 1 == early)
        def _():
            def gather(step, carry):
                line.step(step // groups + 1, step % groups)
                return carry

            lax.fori_loop((early - 1) // 2, steps, gather, 0)
            line.finish()
            l_copy(late_ref, 0, 1 - slot).start()

        @pl.when((pair + 1 < early) & (pair % 2 == 1) & (pair // 2 < steps))
        def _():
            step = pair // 2
            line.step(step // groups + 1, step % groups)

        return carry

    lax.fori_loop(0, pairs, body, 0)
    fill_inverse(low_ref, inverse_ref, sequence)
    block_rows = lat_local // (blocks // devices)

    def rows_copy(bundle):
        return pltpu.make_async_copy(rows_buf.at[bundle], out_ref.at[bundle], out_sem.at[bundle])

    def spread(bundle, carry):
        for turn in range(1, devices):
            source = lax.rem(order + devices - turn, devices)
            got = band_buf.at[bundle, source]
            to_order(got, got, send_sem.at[turn], recv_sem.at[turn, bundle], source).wait_recv()
        got = band_buf.at[bundle, order]
        pltpu.make_async_copy(got, got, own_sem.at[bundle]).wait()
        for device in range(devices):
            for entry in range(share):
                wide_ref[device * share + entry] = band_buf[bundle, device, entry].astype(jnp.float32)

        def turn_row(lat, carry):
            row = (lat // block_rows) * padded + lat % block_rows
            rows_buf[bundle, lat] = wide_ref[:, row].astype(jnp.bfloat16)
            return carry

        lax.fori_loop(0, lat_local, turn_row, 0, unroll=step_of(lat_local, 10))
        rows_copy(bundle).start()
        return carry

    lax.fori_loop(0, sets, spread, 0)
    for turn in range(1, devices):
        peer = lax.rem(order + turn, devices)
        sent = stage_ref.at[:, pl.ds(peer * band, band)]
        to_order(sent, sent, send_sem.at[turn], recv_sem.at[turn, 0], peer).wait_send()
    for bundle in range(sets):
        rows_copy(bundle).wait()


def inverse_kernel(weight_ref, band_ref, table_ref, out_ref):
    sets, steps, _, lanes = band_ref.shape
    samples, _, channels, _ = out_ref.shape
    sc = samples * channels
    pieces = []
    for t in range(steps):
        rows = jnp.concatenate([band_ref[g, t] for g in range(sets)], axis=0)
        pieces.append(jnp.concatenate([rows[:, q * sc : (q + 1) * sc] for q in range(4)], axis=0).T)
    values = jnp.dot(jnp.concatenate(pieces, axis=0), table_ref[...], preferred_element_type=jnp.float32)
    start = pl.program_id(0) * steps
    for t in range(steps):
        scale = weight_ref[start + t] * (2.0 * math.pi / NLON)
        for s in range(samples):
            row = t * sc + s * channels
            out_ref[s, t] = (values[row : row + channels] * scale).astype(jnp.bfloat16)


def body(grad_out, legendre, filter_re, filter_im, quad_weight, pair_order, *, devices, members):
    samples, channels, lat_local, longitudes = grad_out.shape
    pairs, block_rows, packed_rows = legendre.shape
    lanes = 4 * samples * channels
    padded = -(-block_rows // TILE) * TILE
    per_band = lat_local // block_rows
    chips = members // 2
    columns = devices * pairs * 4
    early = (2 * pairs) // 3
    early_groups = step_of(early, 4)
    late_groups = step_of(pairs - early, 2)
    legendre = jnp.pad(legendre, ((0, 0), (0, padded - block_rows), (0, 0)))
    hbm = pl.BlockSpec(memory_space=pl.ANY)
    vmem = pl.BlockSpec(memory_space=pltpu.VMEM)
    smem = pl.BlockSpec(memory_space=pltpu.SMEM)
    bf16 = jnp.bfloat16
    dma = pltpu.SemaphoreType.DMA
    chunks = per_band * padded // TILE
    slack = max(0, (per_band - 1) * block_rows + padded - lat_local)

    def params(collective_id):
        return pltpu.CompilerParams(
            collective_id=collective_id, has_side_effects=True, vmem_limit_bytes=60 << 20
        )

    def line_sems(groups):
        return [dma((chips, groups)), dma((chips, groups)), dma((5,))]

    coeffs, early_table = pl.pallas_call(
        functools.partial(
            forward_kernel, devices=devices, chips=chips, groups=early_groups, block_rows=block_rows
        ),
        in_specs=[smem, hbm, vmem],
        out_specs=[hbm, hbm],
        out_shape=[
            jax.ShapeDtypeStruct((pairs, members, padded, lanes), bf16),
            jax.ShapeDtypeStruct((early, members, padded, packed_rows), bf16),
        ],
        scratch_shapes=[
            pltpu.VMEM((2, samples, TILE + slack, channels, longitudes), bf16),
            pltpu.VMEM((longitudes, -(-columns // 128) * 128), bf16),
            pltpu.VMEM((TILE, columns, -(-(samples * channels) // 128) * 128), jnp.float32),
            pltpu.VMEM((chunks, devices * pairs, TILE, lanes), bf16),
            dma((2,)), dma((devices,)), dma((devices,)), dma, *line_sems(early_groups),
        ],
        compiler_params=params(0),
        name="fourier",
    )(pair_order, jnp.transpose(grad_out, (0, 2, 1, 3)), legendre)

    share = step_of(pairs, 4)
    sets = pairs // share
    sequence = [d * pairs + g * share + j for g in range(sets) for d in range(devices) for j in range(share)]
    rows = per_band * padded
    band, inverse, _ = pl.pallas_call(
        functools.partial(
            middle_kernel, devices=devices, chips=chips, groups=late_groups, samples=samples, sequence=sequence
        ),
        in_specs=[smem, hbm, hbm, vmem, vmem, vmem],
        out_specs=[hbm, vmem, hbm],
        out_shape=[
            jax.ShapeDtypeStruct((sets, lat_local, devices * share, lanes), bf16),
            jax.ShapeDtypeStruct((columns, longitudes), bf16),
            jax.ShapeDtypeStruct((pairs - early, members, padded, packed_rows), bf16),
        ],
        scratch_shapes=[
            pltpu.VMEM((2, members, padded, lanes), bf16),
            pltpu.VMEM((2, members, padded, packed_rows), bf16),
            pltpu.VMEM((HEAD + packed_rows + filter_re.shape[1], 2 * channels), jnp.float32),
            pltpu.VMEM((pairs, members * padded, lanes), bf16),
            pltpu.VMEM((sets, devices, share, rows, lanes), bf16),
            pltpu.VMEM((devices * share, rows, lanes), jnp.float32),
            pltpu.VMEM((sets, lat_local, devices * share, lanes), bf16),
            dma((2,)), dma((2,)), dma((devices,)), dma((devices, sets)), dma((sets,)), dma((sets,)),
            *line_sems(late_groups),
        ],
        compiler_params=params(1),
        name="legendre",
    )(pair_order, coeffs, early_table, legendre, filter_re, filter_im)

    steps = step_of(lat_local, 20)
    values = pl.pallas_call(
        inverse_kernel,
        grid=(lat_local // steps,),
        in_specs=[
            smem,
            pl.BlockSpec((sets, steps, devices * share, lanes), lambda i: (0, i, 0, 0)),
            pl.BlockSpec((columns, longitudes), lambda i: (0, 0)),
        ],
        out_specs=pl.BlockSpec((samples, steps, channels, longitudes), lambda i: (0, i, 0, 0)),
        out_shape=jax.ShapeDtypeStruct((samples, lat_local, channels, longitudes), bf16),
        compiler_params=pltpu.CompilerParams(
            dimension_semantics=("arbitrary",), vmem_limit_bytes=56 << 20
        ),
        name="fourier_back",
    )(quad_weight, band, inverse)
    return jnp.transpose(values, (0, 2, 1, 3))


def solution(mesh):
    in_specs = (
        P(None, "chan", "order", None),
        P("order", "chan", None),
        P("chan", None),
        P("chan", None),
        P("order"),
        P(),
    )
    out_specs = P(None, "chan", "order", None)
    local = functools.partial(body, devices=mesh.shape["order"], members=mesh.shape["chan"])
    return jax.shard_map(local, mesh=mesh, in_specs=in_specs, out_specs=out_specs, check_vma=False)
```

```python
import functools
import math

import jax
import jax.numpy as jnp
from jax import lax
from jax.experimental import pallas as pl
from jax.experimental.pallas import tpu as pltpu
from jax.sharding import PartitionSpec as P

NLON = 1440
M = 720
TILE = 16
FINE = 32
HEAD = 8
MESH = pl.DeviceIdType.MESH


def step_of(count, most):
    return max(d for d in range(1, most + 1) if count % d == 0)


def order_lanes(low_ref, sequence, width):
    count = len(sequence)
    lane = lax.broadcasted_iota(jnp.int32, (1, width), 1)
    turn = sum((lane >= q * count).astype(jnp.int32) for q in range(1, 5))
    place = lane - turn * count
    low = jnp.zeros((1, width), jnp.float32)
    for index, pair in enumerate(sequence):
        low = jnp.where(place == index, low_ref[pair].astype(jnp.float32), low)
    orders = jnp.where(turn < 2, low, (M - 1) - low)
    return orders, (turn == 0) | (turn == 2), turn < 4


def circle(phases):
    phases = phases - NLON * jnp.floor(phases * (1.0 / NLON))
    angles = phases * (2.0 * math.pi / NLON)
    return jnp.cos(angles), jnp.sin(angles)


def iota(shape, axis):
    return lax.broadcasted_iota(jnp.int32, shape, axis).astype(jnp.float32)


def fill_forward(low_ref, table_ref, count):
    width = table_ref.shape[1]
    orders, real, live = order_lanes(low_ref, range(count), width)
    coarse_cos, coarse_sin = circle(iota((NLON // FINE, width), 0) * FINE * orders)
    fine_cos, fine_sin = circle(iota((FINE, width), 0) * orders)
    factor = jnp.where(orders == 0.0, 1.0, 2.0) * jnp.where(live, 1.0, 0.0)
    first = jnp.where(real, coarse_cos, -coarse_sin) * factor
    second = jnp.where(real, -coarse_sin, -coarse_cos) * factor
    for part in range(NLON // FINE):
        rows = first[part : part + 1] * fine_cos + second[part : part + 1] * fine_sin
        table_ref[part * FINE : (part + 1) * FINE] = rows.astype(jnp.bfloat16)


def fill_inverse(low_ref, table_ref, sequence):
    columns = table_ref.shape[0]
    width = -(-columns // 128) * 128
    orders, real, _ = order_lanes(low_ref, sequence, width)
    orders = jnp.broadcast_to(orders, (128, width)).T[:columns]
    real = jnp.broadcast_to(jnp.where(real, 1.0, 0.0), (128, width)).T[:columns] > 0.5
    fine_cos, fine_sin = circle(iota((columns, 128), 1) * orders)
    coarse_cos, coarse_sin = circle(iota((columns, 128), 1) * 128.0 * orders)
    first = jnp.where(real, coarse_cos, -coarse_sin)
    second = jnp.where(real, -coarse_sin, -coarse_cos)
    for start in range(0, NLON, 128):
        part = start // 128
        values = first[:, part : part + 1] * fine_cos + second[:, part : part + 1] * fine_sin
        size = min(128, NLON - start)
        table_ref[:, start : start + size] = values[:, :size].astype(jnp.bfloat16)


class Line:
    def __init__(self, chips, first, pairs, groups, source, table, sems):
        self.chips, self.first, self.pairs, self.groups = chips, first, pairs, groups
        self.source, self.table = source, table
        self.up_recv, self.down_recv, self.flags = sems
        self.index = lax.axis_index("chan")
        self.place = self.index // 2
        self.partner = self.index + 1 - 2 * (self.index % 2)
        self.share = pairs // groups

    def remote(self, src, dst, send, recv, target):
        return pltpu.make_async_remote_copy(
            src_ref=src, dst_ref=dst, send_sem=send, recv_sem=recv, device_id={"chan": target}, device_id_type=MESH
        )

    def own(self):
        src = self.source.at[pl.ds(self.first, self.pairs)]
        return pltpu.make_async_copy(src, self.table.at[:, self.index], self.flags.at[0])

    def start(self):
        self.own().start()
        src = self.source.at[pl.ds(self.first, self.pairs)]
        self.remote(src, self.table.at[:, self.index], self.flags.at[1], self.flags.at[2], self.partner).start()
        for group in range(self.groups):
            src = self.source.at[pl.ds(self.first + group * self.share, self.share)]
            dst = self.table.at[pl.ds(group * self.share, self.share), self.index]

            @pl.when(self.place < self.chips - 1)
            def _():
                self.remote(src, dst, self.flags.at[3], self.up_recv.at[0, group], self.index + 2).start()

            @pl.when(self.place > 0)
            def _():
                self.remote(src, dst, self.flags.at[4], self.down_recv.at[0, group], self.index - 2).start()

    def step(self, hop, group):
        rows = pl.ds(group * self.share, self.share)

        @pl.when(self.place >= hop)
        def _():
            block = self.table.at[rows, self.index - 2 * hop]
            self.remote(block, block, self.flags.at[3], self.up_recv.at[hop - 1, group], self.index - 2).wait_recv()

            @pl.when(self.place < self.chips - 1)
            def _():
                self.remote(block, block, self.flags.at[3], self.up_recv.at[hop, group], self.index + 2).start()

            self.remote(block, block, self.flags.at[1], self.flags.at[2], self.partner).start()

        @pl.when(self.place + hop < self.chips)
        def _():
            block = self.table.at[rows, self.index + 2 * hop]
            self.remote(block, block, self.flags.at[4], self.down_recv.at[hop - 1, group], self.index + 2).wait_recv()

            @pl.when(self.place > 0)
            def _():
                self.remote(block, block, self.flags.at[4], self.down_recv.at[hop, group], self.index - 2).start()

            self.remote(block, block, self.flags.at[1], self.flags.at[2], self.partner).start()

    def finish(self):
        self.own().wait()
        total = self.table.at[:, pl.ds(0, self.chips)]
        every = self.remote(total, total, self.flags.at[1], self.flags.at[2], self.partner)
        every.wait_send()
        every.wait_recv()
        for place in range(self.chips):
            if place < self.chips - 1:

                @pl.when(self.place == place)
                def _():
                    part = self.table.at[:, pl.ds(0, place + 1)]
                    self.remote(part, part, self.flags.at[3], self.flags.at[2], self.partner).wait_send()

            if place > 0:

                @pl.when(self.place == place)
                def _():
                    part = self.table.at[:, pl.ds(0, self.chips - place)]
                    self.remote(part, part, self.flags.at[4], self.flags.at[2], self.partner).wait_send()


def enter(devices, chips):
    order = lax.axis_index("order")
    index = lax.axis_index("chan")
    place = index // 2
    barrier = pltpu.get_barrier_semaphore()
    for turn in range(1, devices):
        peer = lax.rem(order + turn, devices)
        pl.semaphore_signal(barrier, inc=1, device_id={"order": peer}, device_id_type=MESH)
    partner = index + 1 - 2 * (index % 2)
    pl.semaphore_signal(barrier, inc=1, device_id={"chan": partner}, device_id_type=MESH)

    @pl.when(place < chips - 1)
    def _():
        pl.semaphore_signal(barrier, inc=1, device_id={"chan": index + 2}, device_id_type=MESH)

    @pl.when(place > 0)
    def _():
        pl.semaphore_signal(barrier, inc=1, device_id={"chan": index - 2}, device_id_type=MESH)

    near = jnp.minimum(place, 1) + jnp.minimum(chips - 1 - place, 1)
    pl.semaphore_wait(barrier, devices + near)


def to_order(src, dst, send, recv, peer):
    return pltpu.make_async_remote_copy(
        src_ref=src, dst_ref=dst, send_sem=send, recv_sem=recv, device_id={"order": peer}, device_id_type=MESH
    )


def forward_kernel(
    low_ref, x_ref, legendre_ref, out_ref, gathered_ref, x_buf, table_ref, turned_ref, stage_ref,
    x_sem, send_sem, recv_sem, own_sem, up_sem, down_sem, flag_sem, *, devices, chips, groups, block_rows
):
    samples, lat_local, channels, _ = x_ref.shape
    pairs, blocks, padded, lanes = out_ref.shape
    sc = samples * channels
    order = lax.axis_index("order")
    per_band = blocks // devices
    per_block = padded // TILE
    chunks = per_band * per_block
    slack = max(0, (per_band - 1) * block_rows + padded - lat_local)
    line = Line(chips, 0, gathered_ref.shape[0], groups, legendre_ref, gathered_ref, (up_sem, down_sem, flag_sem))

    def x_copy(chunk):
        start = (chunk // per_block) * block_rows + (chunk % per_block) * TILE
        back = jnp.maximum(start + TILE - lat_local, 0)
        slot = chunk % 2
        return pltpu.make_async_copy(
            x_ref.at[:, pl.ds(start - back, TILE)], x_buf.at[slot, :, pl.ds(slack - back, TILE)], x_sem.at[slot]
        )

    x_copy(0).start()
    enter(devices, chips)
    line.start()
    steps = (chips - 1) * groups
    count = devices * pairs
    fill_forward(low_ref, table_ref, count)

    def body(chunk, carry):
        slot = chunk % 2
        x_copy(chunk).wait()

        @pl.when(chunk + 1 < chunks)
        def _():
            x_copy(chunk + 1).start()

        pieces = [x_buf[slot, s, slack + t] for t in range(TILE) for s in range(samples)]
        coeffs = jnp.dot(jnp.concatenate(pieces, axis=0), table_ref[...], preferred_element_type=jnp.float32)
        for t in range(TILE):
            turned = coeffs[t * sc : (t + 1) * sc].T
            turned_ref[t, :, 0:sc] = turned[: turned_ref.shape[1]]
        block, part = chunk // per_block, chunk % per_block
        live = lax.broadcasted_iota(jnp.int32, (TILE, lanes), 0) < block_rows - part * TILE
        for pair in range(count):
            row = jnp.concatenate([turned_ref[:, q * count + pair, 0:sc] for q in range(4)], axis=1)
            stage_ref[chunk, pair] = jnp.where(live, row, 0.0).astype(jnp.bfloat16)
        target = out_ref.at[:, order * per_band + block, pl.ds(part * TILE, TILE)]
        for turn in range(1, devices):
            peer = lax.rem(order + turn, devices)
            src = stage_ref.at[chunk, pl.ds(peer * pairs, pairs)]
            to_order(src, target, send_sem.at[turn], recv_sem.at[turn], peer).start()
        pltpu.make_async_copy(stage_ref.at[chunk, pl.ds(order * pairs, pairs)], target, own_sem).start()
        step = chunk - 1

        @pl.when((step >= 0) & (step < steps))
        def _():
            line.step(step // groups + 1, step % groups)

        return carry

    lax.fori_loop(0, chunks, body, 0)
    if steps > chunks - 1:

        def rest(step, carry):
            line.step(step // groups + 1, step % groups)
            return carry

        lax.fori_loop(chunks - 1, steps, rest, 0)
    for turn in range(1, devices):
        peer = lax.rem(order + turn, devices)
        source = lax.rem(order + devices - turn, devices)
        sent = out_ref.at[:, pl.ds(peer * per_band, per_band)]
        got = out_ref.at[:, pl.ds(source * per_band, per_band)]
        both = to_order(sent, got, send_sem.at[turn], recv_sem.at[turn], peer)
        both.wait_send()
        both.wait_recv()
    own = out_ref.at[:, pl.ds(order * per_band, per_band)]
    pltpu.make_async_copy(own, own, own_sem).wait()
    line.finish()


def middle_kernel(
    low_ref, coeffs_ref, early_ref, legendre_ref, filter_re_ref, filter_im_ref,
    out_ref, last_ref, rest_ref, inverse_ref, late_ref, z_buf, l_buf, gains_ref, stage_ref, band_buf, wide_ref, rows_buf,
    z_sem, l_sem, send_sem, recv_sem, own_sem, out_sem, rest_sem, up_sem, down_sem, flag_sem,
    *, devices, chips, groups, samples, sequence
):
    pairs, blocks, padded, lanes = coeffs_ref.shape
    packed_rows = legendre_ref.shape[2]
    early = early_ref.shape[0]
    rows = blocks * padded
    band = rows // devices
    half = lanes // 2
    sc = half // 2
    channels = sc // samples
    order = lax.axis_index("order")
    line = Line(chips, early, pairs - early, groups, legendre_ref, late_ref, (up_sem, down_sem, flag_sem))

    def z_copy(pair):
        return pltpu.make_async_copy(coeffs_ref.at[pair], z_buf.at[pair % 2], z_sem.at[pair % 2])

    def l_copy(ref, entry, slot):
        return pltpu.make_async_copy(ref.at[entry], l_buf.at[slot], l_sem.at[slot])

    z_copy(0).start()
    l_copy(early_ref, 0, 0).start()
    enter(devices, chips)
    line.start()
    steps = (chips - 1) * groups
    sets, share, lat_local = out_ref.shape[0] + 1, out_ref.shape[2] // devices, out_ref.shape[1]
    head = band - padded
    degrees = filter_re_ref.shape[1]
    filters = jnp.concatenate([filter_re_ref[...], filter_im_ref[...]], axis=0)
    filters = jnp.concatenate([filters, jnp.zeros((2 * channels, packed_rows - degrees), jnp.float32)], axis=1).T
    gains_ref[HEAD : HEAD + packed_rows] = filters
    gains_ref[HEAD + packed_rows :] = jnp.zeros((degrees, 2 * channels), jnp.float32)
    gains_ref[HEAD - 1 : HEAD] = filters[0:1]
    contract = (((0,), (0,)), ((), ()))
    row_ids = lax.broadcasted_iota(jnp.int32, (packed_rows, half), 0)

    def body(pair, carry):
        slot = pair % 2
        z_copy(pair).wait()
        l_copy(early_ref, 0, slot).wait()

        @pl.when(pair + 1 < pairs)
        def _():
            z_copy(pair + 1).start()

        @pl.when(pair + 1 < early)
        def _():
            l_copy(early_ref, pair + 1, 1 - slot).start()

        @pl.when((pair + 1 >= early + 1) & (pair + 1 < pairs))
        def _():
            l_copy(late_ref, pair + 1 - early, 1 - slot).start()

        legendre = l_buf[slot].reshape(rows, packed_rows)
        coeffs = z_buf[slot].reshape(rows, lanes)
        spectrum = lax.dot_general(legendre, coeffs, contract, preferred_element_type=jnp.float32)
        low = low_ref[order * pairs + pair]
        inside = row_ids < M - low
        own = jnp.where(inside, spectrum[:, :half], spectrum[:, half:])
        other = jnp.concatenate([own[:, sc:], own[:, :sc]], axis=1)
        upper = gains_ref[pl.ds(low + HEAD, packed_rows), :]
        gains = jnp.where(inside[:, : 2 * channels], upper, gains_ref[pl.ds(HEAD - 1, packed_rows), :])
        gain_re = gains[:, :channels]
        gain_im = gains[:, channels:]
        gain_re = jnp.concatenate([gain_re] * (2 * samples), axis=1)
        gain_im = jnp.concatenate([gain_im] * samples + [-gain_im] * samples, axis=1)
        filtered = gain_re * own + gain_im * other
        zeros = jnp.zeros_like(filtered)
        split = jnp.concatenate([jnp.where(inside, filtered, zeros), jnp.where(inside, zeros, filtered)], axis=1)
        synthesis = jnp.dot(legendre, split.astype(jnp.bfloat16), preferred_element_type=jnp.float32)
        stage_ref[pair] = synthesis.astype(jnp.bfloat16)
        bundle = pair // share

        def send(size, part):
            target = band_buf.at[bundle, order, pair % share, pl.ds(0, size)]
            for turn in range(1, devices):
                peer = lax.rem(order + turn, devices)
                src = stage_ref.at[pair, pl.ds(peer * band, size)]
                to_order(src, target, send_sem.at[turn, part], recv_sem.at[turn, bundle], peer).start()
            src = stage_ref.at[pair, pl.ds(order * band, size)]
            pltpu.make_async_copy(src, target, own_sem.at[bundle]).start()

        @pl.when(bundle < sets - 1)
        def _():
            send(band, 0)

        @pl.when(bundle == sets - 1)
        def _():
            send(head, 1)
            for device in range(devices):
                src = stage_ref.at[pair, pl.ds(device * band + head, padded)]
                pltpu.make_async_copy(src, rest_ref.at[device, pair % share], rest_sem).start()

        @pl.when(pair + 1 == early)
        def _():
            def gather(step, carry):
                line.step(step // groups + 1, step % groups)
                return carry

            lax.fori_loop((early - 1) // 2, steps, gather, 0)
            line.finish()
            l_copy(late_ref, 0, 1 - slot).start()

        @pl.when((pair + 1 < early) & (pair % 2 == 1) & (pair // 2 < steps))
        def _():
            step = pair // 2
            line.step(step // groups + 1, step % groups)

        return carry

    lax.fori_loop(0, pairs, body, 0)
    fill_inverse(low_ref, inverse_ref, sequence)
    block_rows = lat_local // (blocks // devices)
    early_lat = lat_local - block_rows

    def rows_copy(bundle):
        if bundle is None:
            return pltpu.make_async_copy(rows_buf.at[sets - 1, pl.ds(0, early_lat)], last_ref, out_sem.at[sets - 1])
        return pltpu.make_async_copy(rows_buf.at[bundle], out_ref.at[bundle], out_sem.at[bundle])

    def spread(bundle, size, lats):
        for turn in range(1, devices):
            source = lax.rem(order + devices - turn, devices)
            got = band_buf.at[bundle, source, :, pl.ds(0, size)]
            to_order(got, got, send_sem.at[turn, 0], recv_sem.at[turn, bundle], source).wait_recv()
        got = band_buf.at[bundle, order, :, pl.ds(0, size)]
        pltpu.make_async_copy(got, got, own_sem.at[bundle]).wait()
        for device in range(devices):
            for entry in range(share):
                wide_ref[device * share + entry, 0:size] = band_buf[bundle, device, entry, 0:size].astype(jnp.float32)

        def turn_row(lat, carry):
            row = (lat // block_rows) * padded + lat % block_rows
            rows_buf[bundle, lat] = wide_ref[:, row].astype(jnp.bfloat16)
            return carry

        lax.fori_loop(0, lats, turn_row, 0, unroll=step_of(lats, 10))

    def whole(bundle, carry):
        spread(bundle, band, lat_local)
        rows_copy(bundle).start()
        return carry

    lax.fori_loop(0, sets - 1, whole, 0)
    spread(sets - 1, head, early_lat)
    rows_copy(None).start()
    full = pairs - share
    for turn in range(1, devices):
        peer = lax.rem(order + turn, devices)
        sent = stage_ref.at[pl.ds(0, full), pl.ds(peer * band, band)]
        to_order(sent, sent, send_sem.at[turn, 0], recv_sem.at[turn, 0], peer).wait_send()
        sent = stage_ref.at[pl.ds(full, share), pl.ds(peer * band, head)]
        to_order(sent, sent, send_sem.at[turn, 1], recv_sem.at[turn, 0], peer).wait_send()
    pltpu.make_async_copy(rest_ref, rest_ref, rest_sem).wait()
    for bundle in range(sets - 1):
        rows_copy(bundle).wait()
    rows_copy(None).wait()


def emit(row_sets, start, weight_ref, table_ref, out_ref):
    samples, steps, channels, _ = out_ref.shape
    sc = samples * channels
    pieces = []
    for t in range(steps):
        rows = jnp.concatenate([part(t) for part in row_sets], axis=0)
        pieces.append(jnp.concatenate([rows[:, q * sc : (q + 1) * sc] for q in range(4)], axis=0).T)
    values = jnp.dot(jnp.concatenate(pieces, axis=0), table_ref[...], preferred_element_type=jnp.float32)
    for t in range(steps):
        scale = weight_ref[start + t] * (2.0 * math.pi / NLON)
        for s in range(samples):
            row = t * sc + s * channels
            out_ref[s, t] = (values[row : row + channels] * scale).astype(jnp.bfloat16)


def first_kernel(weight_ref, band_ref, last_ref, table_ref, out_ref):
    row_sets = [functools.partial(lambda g, t: band_ref[g, t], g) for g in range(band_ref.shape[0])]
    row_sets.append(lambda t: last_ref[t])
    emit(row_sets, pl.program_id(0) * out_ref.shape[1], weight_ref, table_ref, out_ref)


def second_kernel(weight_ref, band_ref, rest_ref, table_ref, _, out_ref, wide_ref, *, offset):
    steps = out_ref.shape[1]
    part = pl.program_id(0)

    @pl.when(part == 0)
    def _():
        devices, share, _, _ = rest_ref.shape
        for device in range(devices):
            for entry in range(share):
                wide_ref[device * share + entry] = rest_ref[device, entry].astype(jnp.float32)

    row_sets = [functools.partial(lambda g, t: band_ref[g, t], g) for g in range(band_ref.shape[0])]
    row_sets.append(lambda t: wide_ref[:, part * steps + t].astype(jnp.bfloat16))
    emit(row_sets, offset + part * steps, weight_ref, table_ref, out_ref)


def body(grad_out, legendre, filter_re, filter_im, quad_weight, pair_order, *, devices, members):
    samples, channels, lat_local, longitudes = grad_out.shape
    pairs, block_rows, packed_rows = legendre.shape
    lanes = 4 * samples * channels
    padded = -(-block_rows // TILE) * TILE
    per_band = lat_local // block_rows
    chips = members // 2
    columns = devices * pairs * 4
    early = (2 * pairs) // 3
    early_groups = step_of(early, 4)
    late_groups = step_of(pairs - early, 2)
    legendre = jnp.pad(legendre, ((0, 0), (0, padded - block_rows), (0, 0)))
    hbm = pl.BlockSpec(memory_space=pl.ANY)
    vmem = pl.BlockSpec(memory_space=pltpu.VMEM)
    smem = pl.BlockSpec(memory_space=pltpu.SMEM)
    bf16 = jnp.bfloat16
    dma = pltpu.SemaphoreType.DMA
    chunks = per_band * padded // TILE
    slack = max(0, (per_band - 1) * block_rows + padded - lat_local)

    def params(collective_id):
        return pltpu.CompilerParams(
            collective_id=collective_id, has_side_effects=True, vmem_limit_bytes=60 << 20
        )

    def line_sems(groups):
        return [dma((chips, groups)), dma((chips, groups)), dma((5,))]

    coeffs, early_table = pl.pallas_call(
        functools.partial(
            forward_kernel, devices=devices, chips=chips, groups=early_groups, block_rows=block_rows
        ),
        in_specs=[smem, hbm, vmem],
        out_specs=[hbm, hbm],
        out_shape=[
            jax.ShapeDtypeStruct((pairs, members, padded, lanes), bf16),
            jax.ShapeDtypeStruct((early, members, padded, packed_rows), bf16),
        ],
        scratch_shapes=[
            pltpu.VMEM((2, samples, TILE + slack, channels, longitudes), bf16),
            pltpu.VMEM((longitudes, -(-columns // 128) * 128), bf16),
            pltpu.VMEM((TILE, columns, -(-(samples * channels) // 128) * 128), jnp.float32),
            pltpu.VMEM((chunks, devices * pairs, TILE, lanes), bf16),
            dma((2,)), dma((devices,)), dma((devices,)), dma, *line_sems(early_groups),
        ],
        compiler_params=params(0),
        name="fourier",
    )(pair_order, jnp.transpose(grad_out, (0, 2, 1, 3)), legendre)

    share = step_of(pairs, 4)
    sets = pairs // share
    sequence = [d * pairs + g * share + j for g in range(sets) for d in range(devices) for j in range(share)]
    rows = per_band * padded
    band, last, rest, inverse, _ = pl.pallas_call(
        functools.partial(
            middle_kernel, devices=devices, chips=chips, groups=late_groups, samples=samples, sequence=sequence
        ),
        in_specs=[smem, hbm, hbm, vmem, vmem, vmem],
        out_specs=[hbm, hbm, hbm, vmem, hbm],
        out_shape=[
            jax.ShapeDtypeStruct((sets - 1, lat_local, devices * share, lanes), bf16),
            jax.ShapeDtypeStruct((lat_local - block_rows, devices * share, lanes), bf16),
            jax.ShapeDtypeStruct((devices, share, padded, lanes), bf16),
            jax.ShapeDtypeStruct((columns, longitudes), bf16),
            jax.ShapeDtypeStruct((pairs - early, members, padded, packed_rows), bf16),
        ],
        scratch_shapes=[
            pltpu.VMEM((2, members, padded, lanes), bf16),
            pltpu.VMEM((2, members, padded, packed_rows), bf16),
            pltpu.VMEM((HEAD + packed_rows + filter_re.shape[1], 2 * channels), jnp.float32),
            pltpu.VMEM((pairs, members * padded, lanes), bf16),
            pltpu.VMEM((sets, devices, share, rows, lanes), bf16),
            pltpu.VMEM((devices * share, rows, lanes), jnp.float32),
            pltpu.VMEM((sets, lat_local, devices * share, lanes), bf16),
            dma((2,)), dma((2,)), dma((devices, 2)), dma((devices, sets)), dma((sets,)), dma((sets,)), dma,
            *line_sems(late_groups),
        ],
        compiler_params=params(1),
        name="legendre",
    )(pair_order, coeffs, early_table, legendre, filter_re, filter_im)

    rest = lax.all_to_all(rest, "order", split_axis=0, concat_axis=0, tiled=True)
    steps = step_of(block_rows, 18)
    early_lat = lat_local - block_rows
    ahead = early_lat // steps
    shape = jax.ShapeDtypeStruct((samples, lat_local, channels, longitudes), bf16)
    plain = pltpu.CompilerParams(dimension_semantics=("arbitrary",), vmem_limit_bytes=56 << 20)
    table_block = pl.BlockSpec((columns, longitudes), lambda i: (0, 0))

    def cost(lats):
        return pl.CostEstimate(
            flops=2 * lats * samples * channels * columns * longitudes,
            bytes_accessed=2 * lats * samples * channels * (columns + longitudes),
            transcendentals=0,
        )

    values = pl.pallas_call(
        first_kernel,
        grid=(ahead,),
        in_specs=[
            smem,
            pl.BlockSpec((sets - 1, steps, devices * share, lanes), lambda i: (0, i, 0, 0)),
            pl.BlockSpec((steps, devices * share, lanes), lambda i: (i, 0, 0)),
            table_block,
        ],
        out_specs=pl.BlockSpec((samples, steps, channels, longitudes), lambda i: (0, i, 0, 0)),
        out_shape=shape,
        compiler_params=plain,
        cost_estimate=cost(early_lat),
        name="fourier_back",
    )(quad_weight, band, last, inverse)
    values = pl.pallas_call(
        functools.partial(second_kernel, offset=early_lat),
        grid=(block_rows // steps,),
        in_specs=[
            smem,
            pl.BlockSpec((sets - 1, steps, devices * share, lanes), lambda i: (0, ahead + i, 0, 0)),
            vmem,
            table_block,
            hbm,
        ],
        out_specs=pl.BlockSpec((samples, steps, channels, longitudes), lambda i: (0, ahead + i, 0, 0)),
        out_shape=shape,
        scratch_shapes=[pltpu.VMEM((devices * share, padded, lanes), jnp.float32)],
        input_output_aliases={4: 0},
        compiler_params=plain,
        cost_estimate=cost(block_rows),
        name="fourier_back_rest",
    )(quad_weight, band, rest, inverse, values)
    return jnp.transpose(values, (0, 2, 1, 3))


def solution(mesh):
    in_specs = (
        P(None, "chan", "order", None),
        P("order", "chan", None),
        P("chan", None),
        P("chan", None),
        P("order"),
        P(),
    )
    out_specs = P(None, "chan", "order", None)
    local = functools.partial(body, devices=mesh.shape["order"], members=mesh.shape["chan"])
    return jax.shard_map(local, mesh=mesh, in_specs=in_specs, out_specs=out_specs, check_vma=False)
```

```python
import functools
import math

import jax
import jax.numpy as jnp
from jax import lax
from jax.experimental import pallas as pl
from jax.experimental.pallas import tpu as pltpu
from jax.sharding import PartitionSpec as P

NLON = 1440
M = 720
TILE = 16
FINE = 32
HEAD = 8
MESH = pl.DeviceIdType.MESH


def step_of(count, most):
    return max(d for d in range(1, most + 1) if count % d == 0)


def order_lanes(low_ref, sequence, width):
    count = len(sequence)
    lane = lax.broadcasted_iota(jnp.int32, (1, width), 1)
    turn = sum((lane >= q * count).astype(jnp.int32) for q in range(1, 5))
    place = lane - turn * count
    low = jnp.zeros((1, width), jnp.float32)
    for index, pair in enumerate(sequence):
        low = jnp.where(place == index, low_ref[pair].astype(jnp.float32), low)
    orders = jnp.where(turn < 2, low, (M - 1) - low)
    return orders, (turn == 0) | (turn == 2), turn < 4


def circle(phases):
    phases = phases - NLON * jnp.floor(phases * (1.0 / NLON))
    angles = phases * (2.0 * math.pi / NLON)
    return jnp.cos(angles), jnp.sin(angles)


def iota(shape, axis):
    return lax.broadcasted_iota(jnp.int32, shape, axis).astype(jnp.float32)


def fill_forward(low_ref, table_ref, count):
    width = table_ref.shape[1]
    orders, real, live = order_lanes(low_ref, range(count), width)
    coarse_cos, coarse_sin = circle(iota((NLON // FINE, width), 0) * FINE * orders)
    fine_cos, fine_sin = circle(iota((FINE, width), 0) * orders)
    factor = jnp.where(orders == 0.0, 1.0, 2.0) * jnp.where(live, 1.0, 0.0)
    first = jnp.where(real, coarse_cos, -coarse_sin) * factor
    second = jnp.where(real, -coarse_sin, -coarse_cos) * factor
    for part in range(NLON // FINE):
        rows = first[part : part + 1] * fine_cos + second[part : part + 1] * fine_sin
        table_ref[part * FINE : (part + 1) * FINE] = rows.astype(jnp.bfloat16)


def fill_inverse(low_ref, table_ref, sequence):
    columns = table_ref.shape[0]
    width = -(-columns // 128) * 128
    orders, real, _ = order_lanes(low_ref, sequence, width)
    orders = jnp.broadcast_to(orders, (128, width)).T[:columns]
    real = jnp.broadcast_to(jnp.where(real, 1.0, 0.0), (128, width)).T[:columns] > 0.5
    fine_cos, fine_sin = circle(iota((columns, 128), 1) * orders)
    coarse_cos, coarse_sin = circle(iota((columns, 128), 1) * 128.0 * orders)
    first = jnp.where(real, coarse_cos, -coarse_sin)
    second = jnp.where(real, -coarse_sin, -coarse_cos)
    for start in range(0, NLON, 128):
        part = start // 128
        values = first[:, part : part + 1] * fine_cos + second[:, part : part + 1] * fine_sin
        size = min(128, NLON - start)
        table_ref[:, start : start + size] = values[:, :size].astype(jnp.bfloat16)


class Line:
    def __init__(self, chips, first, pairs, groups, source, table, sems):
        self.chips, self.first, self.pairs, self.groups = chips, first, pairs, groups
        self.source, self.table = source, table
        self.up_recv, self.down_recv, self.flags = sems
        self.index = lax.axis_index("chan")
        self.place = self.index // 2
        self.partner = self.index + 1 - 2 * (self.index % 2)
        self.share = pairs // groups

    def remote(self, src, dst, send, recv, target):
        return pltpu.make_async_remote_copy(
            src_ref=src, dst_ref=dst, send_sem=send, recv_sem=recv, device_id={"chan": target}, device_id_type=MESH
        )

    def own(self):
        src = self.source.at[pl.ds(self.first, self.pairs)]
        return pltpu.make_async_copy(src, self.table.at[:, self.index], self.flags.at[0])

    def start(self):
        self.own().start()
        src = self.source.at[pl.ds(self.first, self.pairs)]
        self.remote(src, self.table.at[:, self.index], self.flags.at[1], self.flags.at[2], self.partner).start()
        for group in range(self.groups):
            src = self.source.at[pl.ds(self.first + group * self.share, self.share)]
            dst = self.table.at[pl.ds(group * self.share, self.share), self.index]

            @pl.when(self.place < self.chips - 1)
            def _():
                self.remote(src, dst, self.flags.at[3], self.up_recv.at[0, group], self.index + 2).start()

            @pl.when(self.place > 0)
            def _():
                self.remote(src, dst, self.flags.at[4], self.down_recv.at[0, group], self.index - 2).start()

    def step(self, hop, group):
        rows = pl.ds(group * self.share, self.share)

        @pl.when(self.place >= hop)
        def _():
            block = self.table.at[rows, self.index - 2 * hop]
            self.remote(block, block, self.flags.at[3], self.up_recv.at[hop - 1, group], self.index - 2).wait_recv()

            @pl.when(self.place < self.chips - 1)
            def _():
                self.remote(block, block, self.flags.at[3], self.up_recv.at[hop, group], self.index + 2).start()

            self.remote(block, block, self.flags.at[1], self.flags.at[2], self.partner).start()

        @pl.when(self.place + hop < self.chips)
        def _():
            block = self.table.at[rows, self.index + 2 * hop]
            self.remote(block, block, self.flags.at[4], self.down_recv.at[hop - 1, group], self.index + 2).wait_recv()

            @pl.when(self.place > 0)
            def _():
                self.remote(block, block, self.flags.at[4], self.down_recv.at[hop, group], self.index - 2).start()

            self.remote(block, block, self.flags.at[1], self.flags.at[2], self.partner).start()

    def finish(self):
        self.own().wait()
        total = self.table.at[:, pl.ds(0, self.chips)]
        every = self.remote(total, total, self.flags.at[1], self.flags.at[2], self.partner)
        every.wait_send()
        every.wait_recv()
        for place in range(self.chips):
            if place < self.chips - 1:

                @pl.when(self.place == place)
                def _():
                    part = self.table.at[:, pl.ds(0, place + 1)]
                    self.remote(part, part, self.flags.at[3], self.flags.at[2], self.partner).wait_send()

            if place > 0:

                @pl.when(self.place == place)
                def _():
                    part = self.table.at[:, pl.ds(0, self.chips - place)]
                    self.remote(part, part, self.flags.at[4], self.flags.at[2], self.partner).wait_send()


def enter(devices, chips):
    order = lax.axis_index("order")
    index = lax.axis_index("chan")
    place = index // 2
    barrier = pltpu.get_barrier_semaphore()
    for turn in range(1, devices):
        peer = lax.rem(order + turn, devices)
        pl.semaphore_signal(barrier, inc=1, device_id={"order": peer}, device_id_type=MESH)
    partner = index + 1 - 2 * (index % 2)
    pl.semaphore_signal(barrier, inc=1, device_id={"chan": partner}, device_id_type=MESH)

    @pl.when(place < chips - 1)
    def _():
        pl.semaphore_signal(barrier, inc=1, device_id={"chan": index + 2}, device_id_type=MESH)

    @pl.when(place > 0)
    def _():
        pl.semaphore_signal(barrier, inc=1, device_id={"chan": index - 2}, device_id_type=MESH)

    near = jnp.minimum(place, 1) + jnp.minimum(chips - 1 - place, 1)
    pl.semaphore_wait(barrier, devices + near)


def to_order(src, dst, send, recv, peer):
    return pltpu.make_async_remote_copy(
        src_ref=src, dst_ref=dst, send_sem=send, recv_sem=recv, device_id={"order": peer}, device_id_type=MESH
    )


def spectral_kernel(
    low_ref, x_ref, legendre_ref, filter_re_ref, filter_im_ref, *refs, devices, chips, groups, block_rows, sequence, sets
):
    out_ref, last_ref, rest_ref, inverse_ref, coeffs_ref = refs[:5]
    tables, refs = refs[5 : 5 + sets], refs[5 + sets :]
    x_buf, table_ref, turned_ref, spent_ref, z_buf, l_buf, gains_ref, stage_ref, band_buf, wide_ref, rows_buf = refs[:11]
    x_sem, there_sem, here_sem, kept_sem, z_sem, l_sem, send_sem, recv_sem, own_sem, out_sem, rest_sem = refs[11:22]
    line_sems = refs[22:]
    samples, lat_local, channels, _ = x_ref.shape
    pairs, blocks, padded, lanes = coeffs_ref.shape
    packed_rows = legendre_ref.shape[2]
    sc = samples * channels
    half = lanes // 2
    share = pairs // sets
    full = pairs - share
    order = lax.axis_index("order")
    per_band = blocks // devices
    per_block = padded // TILE
    chunks = per_band * per_block
    slack = max(0, (per_band - 1) * block_rows + padded - lat_local)
    rows = blocks * padded
    band = rows // devices
    head = band - padded
    early_lat = lat_local - block_rows
    count = devices * pairs
    steps = (chips - 1) * groups
    lines = [
        Line(chips, p * share, share, groups, legendre_ref, tables[p], line_sems[3 * p : 3 * p + 3]) for p in range(sets)
    ]

    def advance(line, first, last):
        def one(step, carry):
            line.step(step // groups + 1, step % groups)
            return carry

        if last > first:
            lax.fori_loop(first, last, one, 0)

    def x_copy(chunk):
        start = (chunk // per_block) * block_rows + (chunk % per_block) * TILE
        back = jnp.maximum(start + TILE - lat_local, 0)
        slot = chunk % 2
        return pltpu.make_async_copy(
            x_ref.at[:, pl.ds(start - back, TILE)], x_buf.at[slot, :, pl.ds(slack - back, TILE)], x_sem.at[slot]
        )

    x_copy(0).start()
    enter(devices, chips)
    for line in lines[:2]:
        line.start()
    fill_forward(low_ref, table_ref, count)

    def give(chunk, first, size, part):
        block = order * per_band + chunk // per_block
        target = coeffs_ref.at[pl.ds(first, size), block, pl.ds((chunk % per_block) * TILE, TILE)]
        for turn in range(1, devices):
            peer = lax.rem(order + turn, devices)
            src = spent_ref.at[chunk, pl.ds(peer * pairs + first, size)]
            to_order(src, target, there_sem.at[turn, part], here_sem.at[turn, part], peer).start()
        src = spent_ref.at[chunk, pl.ds(order * pairs + first, size)]
        pltpu.make_async_copy(src, target, kept_sem.at[part]).start()

    def take(first, size, part):
        for turn in range(1, devices):
            peer = lax.rem(order + turn, devices)
            source = lax.rem(order + devices - turn, devices)
            sent = coeffs_ref.at[pl.ds(first, size), pl.ds(peer * per_band, per_band)]
            got = coeffs_ref.at[pl.ds(first, size), pl.ds(source * per_band, per_band)]
            both = to_order(sent, got, there_sem.at[turn, part], here_sem.at[turn, part], peer)
            both.wait_send()
            both.wait_recv()
        own = coeffs_ref.at[pl.ds(first, size), pl.ds(order * per_band, per_band)]
        pltpu.make_async_copy(own, own, kept_sem.at[part]).wait()

    first_step = chunks // 2 - 1
    inner = min(steps, (chunks - first_step + 1) // 2)

    def analyse(chunk, carry):
        slot = chunk % 2
        x_copy(chunk).wait()

        @pl.when(chunk + 1 < chunks)
        def _():
            x_copy(chunk + 1).start()

        pieces = [x_buf[slot, s, slack + t] for t in range(TILE) for s in range(samples)]
        coeffs = jnp.dot(jnp.concatenate(pieces, axis=0), table_ref[...], preferred_element_type=jnp.float32)
        for t in range(TILE):
            turned = coeffs[t * sc : (t + 1) * sc].T
            turned_ref[t, :, 0:sc] = turned[: turned_ref.shape[1]]
        live = lax.broadcasted_iota(jnp.int32, (TILE, lanes), 0) < block_rows - (chunk % per_block) * TILE
        for pair in range(count):
            row = jnp.concatenate([turned_ref[:, q * count + pair, 0:sc] for q in range(4)], axis=1)
            spent_ref[chunk, pair] = jnp.where(live, row, 0.0).astype(jnp.bfloat16)
        give(chunk, 0, full, 0)
        step = (chunk - first_step) // 2

        @pl.when((chunk >= first_step) & ((chunk - first_step) % 2 == 0) & (step < inner))
        def _():
            lines[0].step(step // groups + 1, step % groups)

        return carry

    lax.fori_loop(0, chunks, analyse, 0)

    def later(chunk, carry):
        give(chunk, full, share, 1)
        return carry

    lax.fori_loop(0, chunks, later, 0)
    degrees = filter_re_ref.shape[1]
    filters = jnp.concatenate([filter_re_ref[...], filter_im_ref[...]], axis=0)
    filters = jnp.concatenate([filters, jnp.zeros((2 * channels, packed_rows - degrees), jnp.float32)], axis=1).T
    gains_ref[HEAD : HEAD + packed_rows] = filters
    gains_ref[HEAD + packed_rows :] = jnp.zeros((degrees, 2 * channels), jnp.float32)
    gains_ref[HEAD - 1 : HEAD] = filters[0:1]
    fill_inverse(low_ref, inverse_ref, sequence)
    contract = (((0,), (0,)), ((), ()))
    row_ids = lax.broadcasted_iota(jnp.int32, (packed_rows, half), 0)

    def z_copy(pair):
        return pltpu.make_async_copy(coeffs_ref.at[pair], z_buf.at[pair % 2], z_sem.at[pair % 2])

    def send(pair, bundle, size, part):
        target = band_buf.at[bundle, order, pair % share, pl.ds(0, size)]
        for turn in range(1, devices):
            peer = lax.rem(order + turn, devices)
            src = stage_ref.at[pair, pl.ds(peer * band, size)]
            to_order(src, target, send_sem.at[turn, part], recv_sem.at[turn, bundle], peer).start()
        src = stage_ref.at[pair, pl.ds(order * band, size)]
        pltpu.make_async_copy(src, target, own_sem.at[bundle]).start()

    def middle(bundle, ahead, first_step):
        base = bundle * share
        table = tables[bundle]

        def l_copy(pair):
            return pltpu.make_async_copy(table.at[pair - base], l_buf.at[pair % 2], l_sem.at[pair % 2])

        z_copy(base).start()
        l_copy(base).start()

        def one(pair, carry):
            slot = pair % 2
            z_copy(pair).wait()
            l_copy(pair).wait()

            @pl.when(pair + 1 < base + share)
            def _():
                z_copy(pair + 1).start()
                l_copy(pair + 1).start()

            legendre = l_buf[slot].reshape(rows, packed_rows)
            coeffs = z_buf[slot].reshape(rows, lanes)
            spectrum = lax.dot_general(legendre, coeffs, contract, preferred_element_type=jnp.float32)
            low = low_ref[order * pairs + pair]
            inside = row_ids < M - low
            own = jnp.where(inside, spectrum[:, :half], spectrum[:, half:])
            other = jnp.concatenate([own[:, sc:], own[:, :sc]], axis=1)
            upper = gains_ref[pl.ds(low + HEAD, packed_rows), :]
            gains = jnp.where(inside[:, : 2 * channels], upper, gains_ref[pl.ds(HEAD - 1, packed_rows), :])
            gain_re = gains[:, :channels]
            gain_im = gains[:, channels:]
            gain_re = jnp.concatenate([gain_re] * (2 * samples), axis=1)
            gain_im = jnp.concatenate([gain_im] * samples + [-gain_im] * samples, axis=1)
            filtered = gain_re * own + gain_im * other
            zeros = jnp.zeros_like(filtered)
            split = jnp.concatenate([jnp.where(inside, filtered, zeros), jnp.where(inside, zeros, filtered)], axis=1)
            synthesis = jnp.dot(legendre, split.astype(jnp.bfloat16), preferred_element_type=jnp.float32)
            stage_ref[pair] = synthesis.astype(jnp.bfloat16)
            if bundle < sets - 1:
                send(pair, bundle, band, 0)
            else:
                send(pair, bundle, head, 1)
                for device in range(devices):
                    src = stage_ref.at[pair, pl.ds(device * band + head, padded)]
                    pltpu.make_async_copy(src, rest_ref.at[device, pair % share], rest_sem).start()
            if ahead is not None:
                step = first_step + (pair - base) // 2

                @pl.when(((pair - base) % 2 == 1) & (step < steps))
                def _():
                    ahead.step(step // groups + 1, step % groups)

            return carry

        lax.fori_loop(base, base + share, one, 0)

    def rows_copy(bundle):
        if bundle == sets - 1:
            return pltpu.make_async_copy(rows_buf.at[pl.ds(0, early_lat)], last_ref, out_sem.at[bundle])
        return pltpu.make_async_copy(rows_buf, out_ref.at[bundle], out_sem.at[bundle])

    def spread(bundle):
        size, lats = (band, lat_local) if bundle < sets - 1 else (head, early_lat)
        for turn in range(1, devices):
            source = lax.rem(order + devices - turn, devices)
            got = band_buf.at[bundle, source, :, pl.ds(0, size)]
            to_order(got, got, send_sem.at[turn, 0], recv_sem.at[turn, bundle], source).wait_recv()
        got = band_buf.at[bundle, order, :, pl.ds(0, size)]
        pltpu.make_async_copy(got, got, own_sem.at[bundle]).wait()
        for device in range(devices):
            for entry in range(share):
                wide_ref[device * share + entry, 0:size] = band_buf[bundle, device, entry, 0:size].astype(jnp.float32)
        if bundle > 0:
            rows_copy(bundle - 1).wait()

        def turn_row(lat, carry):
            row = (lat // block_rows) * padded + lat % block_rows
            rows_buf[lat] = wide_ref[:, row].astype(jnp.bfloat16)
            return carry

        lax.fori_loop(0, lats, turn_row, 0, unroll=step_of(lats, 10))
        rows_copy(bundle).start()

    advance(lines[0], inner, steps)
    lines[0].finish()
    done = min(groups, steps)
    advance(lines[1], 0, done)
    take(0, full, 0)
    for bundle in range(sets):
        if bundle == sets - 1:
            take(full, share, 1)
        ahead = lines[bundle + 1] if bundle + 1 < sets else None
        if bundle == 0:
            middle(bundle, ahead, done)
            done = min(steps, done + share // 2)
        else:
            middle(bundle, None, 0)
            done = 0
        if bundle + 2 < sets:
            lines[bundle + 2].start()
        if ahead is not None:
            if bundle > 0:
                advance(ahead, done, steps - groups)
                done = max(done, steps - groups)
                spread(bundle - 1)
            advance(ahead, done, steps)
            ahead.finish()
        elif bundle > 0:
            spread(bundle - 1)
    spread(sets - 1)
    for turn in range(1, devices):
        peer = lax.rem(order + turn, devices)
        sent = stage_ref.at[pl.ds(0, full), pl.ds(peer * band, band)]
        to_order(sent, sent, send_sem.at[turn, 0], recv_sem.at[turn, 0], peer).wait_send()
        sent = stage_ref.at[pl.ds(full, share), pl.ds(peer * band, head)]
        to_order(sent, sent, send_sem.at[turn, 1], recv_sem.at[turn, 0], peer).wait_send()
    pltpu.make_async_copy(rest_ref, rest_ref, rest_sem).wait()
    rows_copy(sets - 1).wait()


def emit(row_sets, start, weight_ref, table_ref, out_ref):
    samples, steps, channels, _ = out_ref.shape
    sc = samples * channels
    pieces = []
    for t in range(steps):
        rows = jnp.concatenate([part(t) for part in row_sets], axis=0)
        pieces.append(jnp.concatenate([rows[:, q * sc : (q + 1) * sc] for q in range(4)], axis=0).T)
    values = jnp.dot(jnp.concatenate(pieces, axis=0), table_ref[...], preferred_element_type=jnp.float32)
    for t in range(steps):
        scale = weight_ref[start + t] * (2.0 * math.pi / NLON)
        for s in range(samples):
            row = t * sc + s * channels
            out_ref[s, t] = (values[row : row + channels] * scale).astype(jnp.bfloat16)


def first_kernel(weight_ref, band_ref, last_ref, table_ref, out_ref):
    row_sets = [functools.partial(lambda g, t: band_ref[g, t], g) for g in range(band_ref.shape[0])]
    row_sets.append(lambda t: last_ref[t])
    emit(row_sets, pl.program_id(0) * out_ref.shape[1], weight_ref, table_ref, out_ref)


def second_kernel(weight_ref, band_ref, rest_ref, table_ref, _, out_ref, wide_ref, *, offset):
    steps = out_ref.shape[1]
    part = pl.program_id(0)

    @pl.when(part == 0)
    def _():
        devices, share, _, _ = rest_ref.shape
        for device in range(devices):
            for entry in range(share):
                wide_ref[device * share + entry] = rest_ref[device, entry].astype(jnp.float32)

    row_sets = [functools.partial(lambda g, t: band_ref[g, t], g) for g in range(band_ref.shape[0])]
    row_sets.append(lambda t: wide_ref[:, part * steps + t].astype(jnp.bfloat16))
    emit(row_sets, offset + part * steps, weight_ref, table_ref, out_ref)


def body(grad_out, legendre, filter_re, filter_im, quad_weight, pair_order, *, devices, members):
    samples, channels, lat_local, longitudes = grad_out.shape
    pairs, block_rows, packed_rows = legendre.shape
    lanes = 4 * samples * channels
    padded = -(-block_rows // TILE) * TILE
    per_band = lat_local // block_rows
    chips = members // 2
    columns = devices * pairs * 4
    share = step_of(pairs, 4)
    sets = pairs // share
    groups = step_of(share, 2)
    legendre = jnp.pad(legendre, ((0, 0), (0, padded - block_rows), (0, 0)))
    hbm = pl.BlockSpec(memory_space=pl.ANY)
    vmem = pl.BlockSpec(memory_space=pltpu.VMEM)
    smem = pl.BlockSpec(memory_space=pltpu.SMEM)
    bf16 = jnp.bfloat16
    dma = pltpu.SemaphoreType.DMA
    chunks = per_band * padded // TILE
    slack = max(0, (per_band - 1) * block_rows + padded - lat_local)

    sequence = [d * pairs + g * share + j for g in range(sets) for d in range(devices) for j in range(share)]
    rows = per_band * padded
    line = [dma((chips, groups)), dma((chips, groups)), dma((5,))]
    outs = pl.pallas_call(
        functools.partial(
            spectral_kernel, devices=devices, chips=chips, groups=groups, block_rows=block_rows,
            sequence=sequence, sets=sets
        ),
        in_specs=[smem, hbm, vmem, vmem, vmem],
        out_specs=[hbm, hbm, hbm, vmem, hbm] + [hbm] * sets,
        out_shape=[
            jax.ShapeDtypeStruct((sets - 1, lat_local, devices * share, lanes), bf16),
            jax.ShapeDtypeStruct((lat_local - block_rows, devices * share, lanes), bf16),
            jax.ShapeDtypeStruct((devices, share, padded, lanes), bf16),
            jax.ShapeDtypeStruct((columns, longitudes), bf16),
            jax.ShapeDtypeStruct((pairs, members, padded, lanes), bf16),
        ]
        + [jax.ShapeDtypeStruct((share, members, padded, packed_rows), bf16)] * sets,
        scratch_shapes=[
            pltpu.VMEM((2, samples, TILE + slack, channels, longitudes), bf16),
            pltpu.VMEM((longitudes, -(-columns // 128) * 128), bf16),
            pltpu.VMEM((TILE, columns, -(-(samples * channels) // 128) * 128), jnp.float32),
            pltpu.VMEM((chunks, devices * pairs, TILE, lanes), bf16),
            pltpu.VMEM((2, members, padded, lanes), bf16),
            pltpu.VMEM((2, members, padded, packed_rows), bf16),
            pltpu.VMEM((HEAD + packed_rows + filter_re.shape[1], 2 * channels), jnp.float32),
            pltpu.VMEM((pairs, members * padded, lanes), bf16),
            pltpu.VMEM((sets, devices, share, rows, lanes), bf16),
            pltpu.VMEM((devices * share, rows, lanes), jnp.float32),
            pltpu.VMEM((lat_local, devices * share, lanes), bf16),
            dma((2,)), dma((devices, 2)), dma((devices, 2)), dma((2,)), dma((2,)), dma((2,)),
            dma((devices, 2)), dma((devices, sets)), dma((sets,)), dma((sets,)), dma,
            *(line * sets),
        ],
        compiler_params=pltpu.CompilerParams(
            collective_id=0, has_side_effects=True, vmem_limit_bytes=67043328
        ),
        name="spectral",
    )(pair_order, jnp.transpose(grad_out, (0, 2, 1, 3)), legendre, filter_re, filter_im)
    band, last, rest, inverse = outs[:4]

    rest = lax.all_to_all(rest, "order", split_axis=0, concat_axis=0, tiled=True)
    steps = step_of(block_rows, 18)
    early_lat = lat_local - block_rows
    ahead = early_lat // steps
    shape = jax.ShapeDtypeStruct((samples, lat_local, channels, longitudes), bf16)
    plain = pltpu.CompilerParams(dimension_semantics=("arbitrary",), vmem_limit_bytes=56 << 20)
    table_block = pl.BlockSpec((columns, longitudes), lambda i: (0, 0))

    def cost(lats):
        return pl.CostEstimate(
            flops=2 * lats * samples * channels * columns * longitudes,
            bytes_accessed=2 * lats * samples * channels * (columns + longitudes),
            transcendentals=0,
        )

    values = pl.pallas_call(
        first_kernel,
        grid=(ahead,),
        in_specs=[
            smem,
            pl.BlockSpec((sets - 1, steps, devices * share, lanes), lambda i: (0, i, 0, 0)),
            pl.BlockSpec((steps, devices * share, lanes), lambda i: (i, 0, 0)),
            table_block,
        ],
        out_specs=pl.BlockSpec((samples, steps, channels, longitudes), lambda i: (0, i, 0, 0)),
        out_shape=shape,
        compiler_params=plain,
        cost_estimate=cost(early_lat),
        name="fourier_back",
    )(quad_weight, band, last, inverse)
    values = pl.pallas_call(
        functools.partial(second_kernel, offset=early_lat),
        grid=(block_rows // steps,),
        in_specs=[
            smem,
            pl.BlockSpec((sets - 1, steps, devices * share, lanes), lambda i: (0, ahead + i, 0, 0)),
            vmem,
            table_block,
            hbm,
        ],
        out_specs=pl.BlockSpec((samples, steps, channels, longitudes), lambda i: (0, ahead + i, 0, 0)),
        out_shape=shape,
        scratch_shapes=[pltpu.VMEM((devices * share, padded, lanes), jnp.float32)],
        input_output_aliases={4: 0},
        compiler_params=plain,
        cost_estimate=cost(block_rows),
        name="fourier_back_rest",
    )(quad_weight, band, rest, inverse, values)
    return jnp.transpose(values, (0, 2, 1, 3))


def solution(mesh):
    in_specs = (
        P(None, "chan", "order", None),
        P("order", "chan", None),
        P("chan", None),
        P("chan", None),
        P("order"),
        P(),
    )
    out_specs = P(None, "chan", "order", None)
    local = functools.partial(body, devices=mesh.shape["order"], members=mesh.shape["chan"])
    return jax.shard_map(local, mesh=mesh, in_specs=in_specs, out_specs=out_specs, check_vma=False)
```

```python
import functools
import math

import jax
import jax.numpy as jnp
from jax import lax
from jax.experimental import pallas as pl
from jax.experimental.pallas import tpu as pltpu
from jax.sharding import PartitionSpec as P

NLON = 1440
M = 720
TILE = 16
FINE = 32
HEAD = 8
ALIGN = 8
MESH = pl.DeviceIdType.MESH


def step_of(count, most):
    return max(d for d in range(1, most + 1) if count % d == 0)


def order_lanes(low_ref, sequence, width):
    count = len(sequence)
    lane = lax.broadcasted_iota(jnp.int32, (1, width), 1)
    turn = sum((lane >= q * count).astype(jnp.int32) for q in range(1, 5))
    place = lane - turn * count
    low = jnp.zeros((1, width), jnp.float32)
    for index, pair in enumerate(sequence):
        low = jnp.where(place == index, low_ref[pair].astype(jnp.float32), low)
    orders = jnp.where(turn < 2, low, (M - 1) - low)
    return orders, (turn == 0) | (turn == 2), turn < 4


def circle(phases):
    phases = phases - NLON * jnp.floor(phases * (1.0 / NLON))
    angles = phases * (2.0 * math.pi / NLON)
    return jnp.cos(angles), jnp.sin(angles)


def iota(shape, axis):
    return lax.broadcasted_iota(jnp.int32, shape, axis).astype(jnp.float32)


def fill_forward(low_ref, table_ref, count):
    width = table_ref.shape[1]
    orders, real, live = order_lanes(low_ref, range(count), width)
    coarse_cos, coarse_sin = circle(iota((NLON // FINE, width), 0) * FINE * orders)
    fine_cos, fine_sin = circle(iota((FINE, width), 0) * orders)
    factor = jnp.where(orders == 0.0, 1.0, 2.0) * jnp.where(live, 1.0, 0.0)
    first = jnp.where(real, coarse_cos, -coarse_sin) * factor
    second = jnp.where(real, -coarse_sin, -coarse_cos) * factor
    for part in range(NLON // FINE):
        rows = first[part : part + 1] * fine_cos + second[part : part + 1] * fine_sin
        table_ref[part * FINE : (part + 1) * FINE] = rows.astype(jnp.bfloat16)


def fill_inverse(low_ref, table_ref, sequence):
    columns = table_ref.shape[0]
    width = -(-columns // 128) * 128
    orders, real, _ = order_lanes(low_ref, sequence, width)
    orders = jnp.broadcast_to(orders, (128, width)).T[:columns]
    real = jnp.broadcast_to(jnp.where(real, 1.0, 0.0), (128, width)).T[:columns] > 0.5
    fine_cos, fine_sin = circle(iota((columns, 128), 1) * orders)
    coarse_cos, coarse_sin = circle(iota((columns, 128), 1) * 128.0 * orders)
    first = jnp.where(real, coarse_cos, -coarse_sin)
    second = jnp.where(real, -coarse_sin, -coarse_cos)
    for start in range(0, NLON, 128):
        part = start // 128
        values = first[:, part : part + 1] * fine_cos + second[:, part : part + 1] * fine_sin
        size = min(128, NLON - start)
        table_ref[:, start : start + size] = values[:, :size].astype(jnp.bfloat16)


class Line:
    def __init__(self, chips, first, pairs, groups, source, table, sems):
        self.chips, self.first, self.pairs, self.groups = chips, first, pairs, groups
        self.source, self.table = source, table
        self.up_recv, self.down_recv, self.flags = sems
        self.index = lax.axis_index("chan")
        self.place = self.index // 2
        self.partner = self.index + 1 - 2 * (self.index % 2)
        self.share = pairs // groups

    def remote(self, src, dst, send, recv, target):
        return pltpu.make_async_remote_copy(
            src_ref=src, dst_ref=dst, send_sem=send, recv_sem=recv, device_id={"chan": target}, device_id_type=MESH
        )

    def own(self):
        src = self.source.at[pl.ds(self.first, self.pairs)]
        return pltpu.make_async_copy(src, self.table.at[:, self.index], self.flags.at[0])

    def start(self):
        self.own().start()
        src = self.source.at[pl.ds(self.first, self.pairs)]
        self.remote(src, self.table.at[:, self.index], self.flags.at[1], self.flags.at[2], self.partner).start()
        for group in range(self.groups):
            src = self.source.at[pl.ds(self.first + group * self.share, self.share)]
            dst = self.table.at[pl.ds(group * self.share, self.share), self.index]

            @pl.when(self.place < self.chips - 1)
            def _():
                self.remote(src, dst, self.flags.at[3], self.up_recv.at[0, group], self.index + 2).start()

            @pl.when(self.place > 0)
            def _():
                self.remote(src, dst, self.flags.at[4], self.down_recv.at[0, group], self.index - 2).start()

    def step(self, hop, group):
        rows = pl.ds(group * self.share, self.share)

        @pl.when(self.place >= hop)
        def _():
            block = self.table.at[rows, self.index - 2 * hop]
            self.remote(block, block, self.flags.at[3], self.up_recv.at[hop - 1, group], self.index - 2).wait_recv()

            @pl.when(self.place < self.chips - 1)
            def _():
                self.remote(block, block, self.flags.at[3], self.up_recv.at[hop, group], self.index + 2).start()

            self.remote(block, block, self.flags.at[1], self.flags.at[2], self.partner).start()

        @pl.when(self.place + hop < self.chips)
        def _():
            block = self.table.at[rows, self.index + 2 * hop]
            self.remote(block, block, self.flags.at[4], self.down_recv.at[hop - 1, group], self.index + 2).wait_recv()

            @pl.when(self.place > 0)
            def _():
                self.remote(block, block, self.flags.at[4], self.down_recv.at[hop, group], self.index - 2).start()

            self.remote(block, block, self.flags.at[1], self.flags.at[2], self.partner).start()

    def finish(self):
        self.own().wait()
        total = self.table.at[:, pl.ds(0, self.chips)]
        every = self.remote(total, total, self.flags.at[1], self.flags.at[2], self.partner)
        every.wait_send()
        every.wait_recv()
        for place in range(self.chips):
            if place < self.chips - 1:

                @pl.when(self.place == place)
                def _():
                    part = self.table.at[:, pl.ds(0, place + 1)]
                    self.remote(part, part, self.flags.at[3], self.flags.at[2], self.partner).wait_send()

            if place > 0:

                @pl.when(self.place == place)
                def _():
                    part = self.table.at[:, pl.ds(0, self.chips - place)]
                    self.remote(part, part, self.flags.at[4], self.flags.at[2], self.partner).wait_send()


def enter(devices, chips):
    order = lax.axis_index("order")
    index = lax.axis_index("chan")
    place = index // 2
    barrier = pltpu.get_barrier_semaphore()
    for turn in range(1, devices):
        peer = lax.rem(order + turn, devices)
        pl.semaphore_signal(barrier, inc=1, device_id={"order": peer}, device_id_type=MESH)
    partner = index + 1 - 2 * (index % 2)
    pl.semaphore_signal(barrier, inc=1, device_id={"chan": partner}, device_id_type=MESH)

    @pl.when(place < chips - 1)
    def _():
        pl.semaphore_signal(barrier, inc=1, device_id={"chan": index + 2}, device_id_type=MESH)

    @pl.when(place > 0)
    def _():
        pl.semaphore_signal(barrier, inc=1, device_id={"chan": index - 2}, device_id_type=MESH)

    near = jnp.minimum(place, 1) + jnp.minimum(chips - 1 - place, 1)
    pl.semaphore_wait(barrier, devices + near)


def to_order(src, dst, send, recv, peer):
    return pltpu.make_async_remote_copy(
        src_ref=src, dst_ref=dst, send_sem=send, recv_sem=recv, device_id={"order": peer}, device_id_type=MESH
    )


def spectral_kernel(
    low_ref, x_ref, block_ref, filter_re_ref, filter_im_ref, *refs, devices, chips, groups, block_rows, sequence, sets
):
    out_ref, last_ref, rest_ref, inverse_ref, coeffs_ref = refs[:5]
    tables, refs = refs[5 : 5 + sets], refs[5 + sets :]
    legendre_ref, end_ref, ends_ref, end_buf, refs = *refs[:4], refs[4:]
    x_buf, table_ref, turned_ref, spent_ref, z_buf, l_buf, gains_ref, stage_ref, band_buf, wide_ref, rows_buf = refs[:11]
    x_sem, there_sem, here_sem, kept_sem, z_sem, l_sem, send_sem, recv_sem, own_sem, out_sem, rest_sem = refs[11:22]
    line_sems = refs[22:]
    samples, lat_local, channels, _ = x_ref.shape
    pairs, _, packed, lanes = coeffs_ref.shape
    _, blocks, padded, packed_rows = l_buf.shape
    sc = samples * channels
    half = lanes // 2
    main, ends = padded - ALIGN, end_ref.shape[2]
    tail = block_rows - main
    share = pairs // sets
    full = pairs - share
    order = lax.axis_index("order")
    per_band = blocks // devices
    per_block = padded // TILE
    chunks = per_band * per_block
    slack = max(0, (per_band - 1) * block_rows + padded - lat_local)
    rows = blocks * padded
    band = rows // devices
    head = band - padded
    early_lat = lat_local - block_rows
    count = devices * pairs
    steps = (chips - 1) * groups
    lines = [
        Line(chips, p * share, share, groups, legendre_ref, tables[p], line_sems[3 * p : 3 * p + 3]) for p in range(sets)
    ]

    def advance(line, first, last):
        def one(step, carry):
            line.step(step // groups + 1, step % groups)
            return carry

        if last > first:
            lax.fori_loop(first, last, one, 0)

    def x_copy(chunk):
        start = (chunk // per_block) * block_rows + (chunk % per_block) * TILE
        back = jnp.maximum(start + TILE - lat_local, 0)
        slot = chunk % 2
        return pltpu.make_async_copy(
            x_ref.at[:, pl.ds(start - back, TILE)], x_buf.at[slot, :, pl.ds(slack - back, TILE)], x_sem.at[slot]
        )

    x_copy(0).start()
    enter(devices, chips)
    for pair in range(pairs):
        legendre_ref[pair, 0:main] = block_ref[pair, 0:main]
        rows_left = block_ref[pair, main:block_rows].astype(jnp.float32)
        rows_left = jnp.concatenate([rows_left, jnp.zeros((padded - block_rows, packed_rows), jnp.float32)], axis=0)
        legendre_ref[pair, main:padded] = rows_left.astype(jnp.bfloat16)
    for line in lines[:2]:
        line.start()
    fill_forward(low_ref, table_ref, count)

    def give_rows(source_ref, entry, place, size, first, number, part):
        target = coeffs_ref.at[pl.ds(first, number), order, pl.ds(place, size)]
        for turn in range(1, devices):
            peer = lax.rem(order + turn, devices)
            src = source_ref.at[entry, pl.ds(peer * pairs + first, number), pl.ds(0, size)]
            to_order(src, target, there_sem.at[turn, part], here_sem.at[turn, part], peer).start()
        src = source_ref.at[entry, pl.ds(order * pairs + first, number), pl.ds(0, size)]
        pltpu.make_async_copy(src, target, kept_sem.at[part]).start()

    def give(chunk, first, number, part):
        within = chunk % per_block
        place = (chunk // per_block) * main + within * TILE

        @pl.when(within < per_block - 1)
        def _():
            give_rows(spent_ref, chunk, place, TILE, first, number, part)

        @pl.when(within == per_block - 1)
        def _():
            give_rows(spent_ref, chunk, place, main - (per_block - 1) * TILE, first, number, part)

    def give_ends(first, number, part):
        give_rows(end_ref, 0, per_band * main, ends, first, number, part)

    def take(first, number, part):
        for turn in range(1, devices):
            peer = lax.rem(order + turn, devices)
            source = lax.rem(order + devices - turn, devices)
            sent = coeffs_ref.at[pl.ds(first, number), peer]
            got = coeffs_ref.at[pl.ds(first, number), source]
            both = to_order(sent, got, there_sem.at[turn, part], here_sem.at[turn, part], peer)
            both.wait_send()
            both.wait_recv()
        own = coeffs_ref.at[pl.ds(first, number), order]
        pltpu.make_async_copy(own, own, kept_sem.at[part]).wait()

    first_step = chunks // 2 - 1
    inner = min(steps, (chunks - first_step + 1) // 2)

    def analyse(chunk, carry):
        slot = chunk % 2
        x_copy(chunk).wait()

        @pl.when(chunk + 1 < chunks)
        def _():
            x_copy(chunk + 1).start()

        pieces = [x_buf[slot, s, slack + t] for t in range(TILE) for s in range(samples)]
        coeffs = jnp.dot(jnp.concatenate(pieces, axis=0), table_ref[...], preferred_element_type=jnp.float32)
        for t in range(TILE):
            turned = coeffs[t * sc : (t + 1) * sc].T
            turned_ref[t, :, 0:sc] = turned[: turned_ref.shape[1]]
        live = lax.broadcasted_iota(jnp.int32, (TILE, lanes), 0) < block_rows - (chunk % per_block) * TILE
        for pair in range(count):
            row = jnp.concatenate([turned_ref[:, q * count + pair, 0:sc] for q in range(4)], axis=1)
            spent_ref[chunk, pair] = jnp.where(live, row, 0.0).astype(jnp.bfloat16)
        give(chunk, 0, full, 0)
        step = (chunk - first_step) // 2

        @pl.when((chunk >= first_step) & ((chunk - first_step) % 2 == 0) & (step < inner))
        def _():
            lines[0].step(step // groups + 1, step % groups)

        return carry

    lax.fori_loop(0, chunks, analyse, 0)

    def collect(pair, carry):
        last = main - (per_block - 1) * TILE
        pieces = []
        for block in range(per_band):
            rows_left = spent_ref[block * per_block + per_block - 1, pair].astype(jnp.float32)
            pieces.append(rows_left[last : last + tail])
        pieces.append(jnp.zeros((ends - per_band * tail, lanes), jnp.float32))
        end_ref[0, pair] = jnp.concatenate(pieces, axis=0).astype(jnp.bfloat16)
        return carry

    lax.fori_loop(0, count, collect, 0)
    give_ends(0, full, 0)
    give_ends(full, share, 1)

    def later(chunk, carry):
        give(chunk, full, share, 1)
        return carry

    lax.fori_loop(0, chunks, later, 0)
    degrees = filter_re_ref.shape[1]
    filters = jnp.concatenate([filter_re_ref[...], filter_im_ref[...]], axis=0)
    filters = jnp.concatenate([filters, jnp.zeros((2 * channels, packed_rows - degrees), jnp.float32)], axis=1).T
    gains_ref[HEAD : HEAD + packed_rows] = filters
    gains_ref[HEAD + packed_rows :] = jnp.zeros((degrees, 2 * channels), jnp.float32)
    gains_ref[HEAD - 1 : HEAD] = filters[0:1]
    fill_inverse(low_ref, inverse_ref, sequence)
    contract = (((0,), (0,)), ((), ()))
    row_ids = lax.broadcasted_iota(jnp.int32, (packed_rows, half), 0)

    class Loads:
        def __init__(self, pair):
            slot = pair % 2
            source = coeffs_ref.at[pair]
            self.copies = [
                pltpu.make_async_copy(
                    source.at[:, pl.ds(block * main, main)], z_buf.at[slot, :, block, pl.ds(0, main)], z_sem.at[slot, block]
                )
                for block in range(per_band)
            ]
            last = source.at[:, pl.ds(per_band * main, ends)]
            self.copies.append(pltpu.make_async_copy(last, end_buf.at[slot], z_sem.at[slot, per_band]))

        def start(self):
            for copy in self.copies:
                copy.start()

        def wait(self):
            for copy in self.copies:
                copy.wait()

    def z_copy(pair):
        return Loads(pair)

    def pass_on(src_of, target, bundle, part):
        for turn in range(1, devices):
            peer = lax.rem(order + turn, devices)
            to_order(src_of(peer), target, send_sem.at[turn, part], recv_sem.at[turn, bundle], peer).start()
        pltpu.make_async_copy(src_of(order), target, own_sem.at[bundle]).start()

    def send(pair, bundle):
        target = band_buf.at[bundle, order, pair % share]
        if bundle == sets - 1:
            pass_on(lambda d: stage_ref.at[pair, pl.ds(d * band, head)], target.at[pl.ds(0, head)], bundle, 1)
            return
        for block in range(per_band):
            pass_on(
                lambda d: stage_ref.at[pair, pl.ds(d * band + block * padded, main)],
                target.at[pl.ds(block * main, main)], bundle, 0,
            )
        pass_on(lambda d: ends_ref.at[pair, d], target.at[pl.ds(per_band * main, ends)], bundle, 0)

    def middle(bundle, ahead, first_step):
        base = bundle * share
        table = tables[bundle]

        def l_copy(pair):
            return pltpu.make_async_copy(table.at[pair - base], l_buf.at[pair % 2], l_sem.at[pair % 2])

        z_copy(base).start()
        l_copy(base).start()

        def one(pair, carry):
            slot = pair % 2
            z_copy(pair).wait()
            l_copy(pair).wait()

            @pl.when(pair + 1 < base + share)
            def _():
                z_copy(pair + 1).start()
                l_copy(pair + 1).start()

            legendre = l_buf[slot].reshape(rows, packed_rows)
            for device in range(devices):
                rows_left = end_buf[slot, device].astype(jnp.float32)
                for block in range(per_band):
                    piece = rows_left[block * tail : (block + 1) * tail]
                    piece = jnp.concatenate([piece, jnp.zeros((ALIGN - tail, lanes), jnp.float32)], axis=0)
                    z_buf[slot, device, block, main:padded] = piece.astype(jnp.bfloat16)
            coeffs = z_buf[slot].reshape(rows, lanes)
            spectrum = lax.dot_general(legendre, coeffs, contract, preferred_element_type=jnp.float32)
            low = low_ref[order * pairs + pair]
            inside = row_ids < M - low
            own = jnp.where(inside, spectrum[:, :half], spectrum[:, half:])
            other = jnp.concatenate([own[:, sc:], own[:, :sc]], axis=1)
            upper = gains_ref[pl.ds(low + HEAD, packed_rows), :]
            gains = jnp.where(inside[:, : 2 * channels], upper, gains_ref[pl.ds(HEAD - 1, packed_rows), :])
            gain_re = gains[:, :channels]
            gain_im = gains[:, channels:]
            gain_re = jnp.concatenate([gain_re] * (2 * samples), axis=1)
            gain_im = jnp.concatenate([gain_im] * samples + [-gain_im] * samples, axis=1)
            filtered = gain_re * own + gain_im * other
            zeros = jnp.zeros_like(filtered)
            split = jnp.concatenate([jnp.where(inside, filtered, zeros), jnp.where(inside, zeros, filtered)], axis=1)
            synthesis = jnp.dot(legendre, split.astype(jnp.bfloat16), preferred_element_type=jnp.float32)
            stage_ref[pair] = synthesis.astype(jnp.bfloat16)
            if bundle < sets - 1:
                for device in range(devices):
                    starts = [device * band + block * padded + main for block in range(per_band)]
                    pieces = [synthesis[start : start + tail] for start in starts]
                    pieces.append(jnp.zeros((ends - per_band * tail, lanes), jnp.float32))
                    ends_ref[pair, device] = jnp.concatenate(pieces, axis=0).astype(jnp.bfloat16)
            send(pair, bundle)
            if bundle == sets - 1:
                for device in range(devices):
                    src = stage_ref.at[pair, pl.ds(device * band + head, padded)]
                    pltpu.make_async_copy(src, rest_ref.at[device, pair % share], rest_sem).start()
            if ahead is not None:
                step = first_step + (pair - base) // 2

                @pl.when(((pair - base) % 2 == 1) & (step < steps))
                def _():
                    ahead.step(step // groups + 1, step % groups)

            return carry

        lax.fori_loop(base, base + share, one, 0)

    def rows_copy(bundle):
        if bundle == sets - 1:
            return pltpu.make_async_copy(rows_buf.at[pl.ds(0, early_lat)], last_ref, out_sem.at[bundle])
        return pltpu.make_async_copy(rows_buf, out_ref.at[bundle], out_sem.at[bundle])

    def spread(bundle):
        size, lats = (packed, lat_local) if bundle < sets - 1 else (head, early_lat)
        for turn in range(1, devices):
            source = lax.rem(order + devices - turn, devices)
            got = band_buf.at[bundle, source, :, pl.ds(0, size)]
            to_order(got, got, send_sem.at[turn, 0], recv_sem.at[turn, bundle], source).wait_recv()
        got = band_buf.at[bundle, order, :, pl.ds(0, size)]
        pltpu.make_async_copy(got, got, own_sem.at[bundle]).wait()
        for device in range(devices):
            for entry in range(share):
                wide_ref[device * share + entry, 0:size] = band_buf[bundle, device, entry, 0:size].astype(jnp.float32)
        if bundle > 0:
            rows_copy(bundle - 1).wait()

        def turn_row(lat, carry):
            block, within = lat // block_rows, lat % block_rows
            if bundle < sets - 1:
                over = jnp.maximum(within - main + 1, 0)
                past = jnp.minimum(over, 1)
                row = (1 - past) * (block * main + within) + past * (per_band * main + block * tail + over - 1)
            else:
                row = block * padded + within
            rows_buf[lat] = wide_ref[:, row].astype(jnp.bfloat16)
            return carry

        lax.fori_loop(0, lats, turn_row, 0, unroll=step_of(lats, 10))
        rows_copy(bundle).start()

    advance(lines[0], inner, steps)
    lines[0].finish()
    done = min(groups, steps)
    advance(lines[1], 0, done)
    take(0, full, 0)
    for bundle in range(sets):
        if bundle == sets - 1:
            take(full, share, 1)
        ahead = lines[bundle + 1] if bundle + 1 < sets else None
        if bundle == 0:
            middle(bundle, ahead, done)
            done = min(steps, done + share // 2)
        else:
            middle(bundle, None, 0)
            done = 0
        if bundle + 2 < sets:
            lines[bundle + 2].start()
        if ahead is not None:
            if bundle > 0:
                advance(ahead, done, steps - groups)
                done = max(done, steps - groups)
                spread(bundle - 1)
            advance(ahead, done, steps)
            ahead.finish()
        elif bundle > 0:
            spread(bundle - 1)
    spread(sets - 1)
    for turn in range(1, devices):
        peer = lax.rem(order + turn, devices)
        sent = band_buf.at[pl.ds(0, sets - 1), peer]
        to_order(sent, sent, send_sem.at[turn, 0], recv_sem.at[turn, 0], peer).wait_send()
        sent = band_buf.at[sets - 1, peer, :, pl.ds(0, head)]
        to_order(sent, sent, send_sem.at[turn, 1], recv_sem.at[turn, 0], peer).wait_send()
    pltpu.make_async_copy(rest_ref, rest_ref, rest_sem).wait()
    rows_copy(sets - 1).wait()


def emit(row_sets, start, weight_ref, table_ref, out_ref):
    samples, steps, channels, _ = out_ref.shape
    sc = samples * channels
    pieces = []
    for t in range(steps):
        rows = jnp.concatenate([part(t) for part in row_sets], axis=0)
        pieces.append(jnp.concatenate([rows[:, q * sc : (q + 1) * sc] for q in range(4)], axis=0).T)
    values = jnp.dot(jnp.concatenate(pieces, axis=0), table_ref[...], preferred_element_type=jnp.float32)
    for t in range(steps):
        scale = weight_ref[start + t] * (2.0 * math.pi / NLON)
        for s in range(samples):
            row = t * sc + s * channels
            out_ref[s, t] = (values[row : row + channels] * scale).astype(jnp.bfloat16)


def first_kernel(weight_ref, band_ref, last_ref, table_ref, out_ref):
    row_sets = [functools.partial(lambda g, t: band_ref[g, t], g) for g in range(band_ref.shape[0])]
    row_sets.append(lambda t: last_ref[t])
    emit(row_sets, pl.program_id(0) * out_ref.shape[1], weight_ref, table_ref, out_ref)


def second_kernel(weight_ref, band_ref, source_ref, table_ref, _, out_ref, rest_ref, wide_ref, sem, *, offset):
    steps = out_ref.shape[1]
    part = pl.program_id(0)

    @pl.when(part == 0)
    def _():
        copy = pltpu.make_async_copy(source_ref, rest_ref, sem)
        copy.start()
        copy.wait()
        devices, share, _, _ = rest_ref.shape
        for device in range(devices):
            for entry in range(share):
                wide_ref[device * share + entry] = rest_ref[device, entry].astype(jnp.float32)

    row_sets = [functools.partial(lambda g, t: band_ref[g, t], g) for g in range(band_ref.shape[0])]
    row_sets.append(lambda t: wide_ref[:, part * steps + t].astype(jnp.bfloat16))
    emit(row_sets, offset + part * steps, weight_ref, table_ref, out_ref)


def body(grad_out, legendre, filter_re, filter_im, quad_weight, pair_order, *, devices, members):
    samples, channels, lat_local, longitudes = grad_out.shape
    pairs, block_rows, packed_rows = legendre.shape
    lanes = 4 * samples * channels
    padded = -(-block_rows // TILE) * TILE
    per_band = lat_local // block_rows
    chips = members // 2
    columns = devices * pairs * 4
    share = step_of(pairs, 4)
    sets = pairs // share
    groups = step_of(share, 2)
    main = padded - ALIGN
    ends = -(-per_band * (block_rows - main) // ALIGN) * ALIGN
    packed = per_band * main + ends
    hbm = pl.BlockSpec(memory_space=pl.ANY)
    vmem = pl.BlockSpec(memory_space=pltpu.VMEM)
    smem = pl.BlockSpec(memory_space=pltpu.SMEM)
    bf16 = jnp.bfloat16
    dma = pltpu.SemaphoreType.DMA
    chunks = per_band * padded // TILE
    slack = max(0, (per_band - 1) * block_rows + padded - lat_local)

    sequence = [d * pairs + g * share + j for g in range(sets) for d in range(devices) for j in range(share)]
    line = [dma((chips, groups)), dma((chips, groups)), dma((5,))]
    outs = pl.pallas_call(
        functools.partial(
            spectral_kernel, devices=devices, chips=chips, groups=groups, block_rows=block_rows,
            sequence=sequence, sets=sets
        ),
        in_specs=[smem, hbm, vmem, vmem, vmem],
        out_specs=[hbm, hbm, hbm, vmem, hbm] + [hbm] * sets,
        out_shape=[
            jax.ShapeDtypeStruct((sets - 1, lat_local, devices * share, lanes), bf16),
            jax.ShapeDtypeStruct((lat_local - block_rows, devices * share, lanes), bf16),
            jax.ShapeDtypeStruct((devices, share, padded, lanes), bf16),
            jax.ShapeDtypeStruct((columns, longitudes), bf16),
            jax.ShapeDtypeStruct((pairs, devices, packed, lanes), bf16),
        ]
        + [jax.ShapeDtypeStruct((share, members, padded, packed_rows), bf16)] * sets,
        scratch_shapes=[
            pltpu.VMEM((pairs, padded, packed_rows), bf16),
            pltpu.VMEM((1, devices * pairs, ends, lanes), bf16),
            pltpu.VMEM((pairs, devices, ends, lanes), bf16),
            pltpu.VMEM((2, devices, ends, lanes), bf16),
            pltpu.VMEM((2, samples, TILE + slack, channels, longitudes), bf16),
            pltpu.VMEM((longitudes, -(-columns // 128) * 128), bf16),
            pltpu.VMEM((TILE, columns, -(-(samples * channels) // 128) * 128), jnp.float32),
            pltpu.VMEM((chunks, devices * pairs, TILE, lanes), bf16),
            pltpu.VMEM((2, devices, per_band, padded, lanes), bf16),
            pltpu.VMEM((2, members, padded, packed_rows), bf16),
            pltpu.VMEM((HEAD + packed_rows + filter_re.shape[1], 2 * channels), jnp.float32),
            pltpu.VMEM((pairs, members * padded, lanes), bf16),
            pltpu.VMEM((sets, devices, share, packed, lanes), bf16),
            pltpu.VMEM((devices * share, packed, lanes), jnp.float32),
            pltpu.VMEM((lat_local, devices * share, lanes), bf16),
            dma((2,)), dma((devices, 2)), dma((devices, 2)), dma((2,)), dma((2, per_band + 1)), dma((2,)),
            dma((devices, 2)), dma((devices, sets)), dma((sets,)), dma((sets,)), dma,
            *(line * sets),
        ],
        compiler_params=pltpu.CompilerParams(
            collective_id=0, has_side_effects=True, vmem_limit_bytes=67043328
        ),
        name="spectral",
    )(pair_order, jnp.transpose(grad_out, (0, 2, 1, 3)), legendre, filter_re, filter_im)
    band, last, rest, inverse = outs[:4]

    rest = lax.all_to_all(rest, "order", split_axis=0, concat_axis=0, tiled=True)
    steps = step_of(block_rows, 18)
    early_lat = lat_local - block_rows
    ahead = early_lat // steps
    shape = jax.ShapeDtypeStruct((samples, lat_local, channels, longitudes), bf16)
    plain = pltpu.CompilerParams(dimension_semantics=("arbitrary",), vmem_limit_bytes=56 << 20)
    table_block = pl.BlockSpec((columns, longitudes), lambda i: (0, 0))

    def cost(lats):
        return pl.CostEstimate(
            flops=2 * lats * samples * channels * columns * longitudes,
            bytes_accessed=2 * lats * samples * channels * (columns + longitudes),
            transcendentals=0,
        )

    values = pl.pallas_call(
        first_kernel,
        grid=(ahead,),
        in_specs=[
            smem,
            pl.BlockSpec((sets - 1, steps, devices * share, lanes), lambda i: (0, i, 0, 0)),
            pl.BlockSpec((steps, devices * share, lanes), lambda i: (i, 0, 0)),
            table_block,
        ],
        out_specs=pl.BlockSpec((samples, steps, channels, longitudes), lambda i: (0, i, 0, 0)),
        out_shape=shape,
        compiler_params=plain,
        cost_estimate=cost(early_lat),
        name="fourier_back",
    )(quad_weight, band, last, inverse)
    values = pl.pallas_call(
        functools.partial(second_kernel, offset=early_lat),
        grid=(block_rows // steps,),
        in_specs=[
            smem,
            pl.BlockSpec((sets - 1, steps, devices * share, lanes), lambda i: (0, ahead + i, 0, 0)),
            hbm,
            table_block,
            hbm,
        ],
        out_specs=pl.BlockSpec((samples, steps, channels, longitudes), lambda i: (0, ahead + i, 0, 0)),
        out_shape=shape,
        scratch_shapes=[
            pltpu.VMEM((devices, share, padded, lanes), bf16),
            pltpu.VMEM((devices * share, padded, lanes), jnp.float32),
            dma,
        ],
        input_output_aliases={4: 0},
        compiler_params=plain,
        cost_estimate=cost(block_rows),
        name="fourier_back_rest",
    )(quad_weight, band, rest, inverse, values)
    return jnp.transpose(values, (0, 2, 1, 3))


def solution(mesh):
    in_specs = (
        P(None, "chan", "order", None),
        P("order", "chan", None),
        P("chan", None),
        P("chan", None),
        P("order"),
        P(),
    )
    out_specs = P(None, "chan", "order", None)
    local = functools.partial(body, devices=mesh.shape["order"], members=mesh.shape["chan"])
    return jax.shard_map(local, mesh=mesh, in_specs=in_specs, out_specs=out_specs, check_vma=False)
```
